256 devices in a mesh: tm: 32 (over x, y, core), space: 8 (over z).
Axes of the slice: x: 4, y: 4, z: 8, core: 2. Of those that a mesh axis runs over, the one named last changes fastest.
Arguments:
- starts: float32 [32, 128, 16, 256], P('tm', 'space'), may hold values from -6 to 6
- east_velocity: float32 [128, 16, 256], P('space'), may hold values from -0.3 to 0.3
- vertical_velocity: float32 [128, 16, 256], P('space'), may hold values from -0.05 to 0.05
- north_velocity: float32 [128, 16, 256], P('space'), may hold values from -0.1 to 0.1
- class_map: int32 [128, 16, 256], P('space'), may hold values from 0 to 7
- land_mask: int32 [128, 16, 256], P('space'), may hold values 0 or 1
- class_diffusivity: float32 [8], replicated, may hold values from 0.005 to 0.08
Outputs:
- new_ends: float32 [32, 128, 16, 256], P('tm', 'space')
The draws below stay inside these ranges and needn't reach their ends.
All inputs are finite; a program needn't handle non-finite values. No bound on the sum of `land_mask` on one device may be relied on, other than what follows from the above.
Results may differ from the reference program's by a relative error of at most 0.00002.
Values sent between devices are 32-bit elements; how exact they have to be, the bound alone decides.
A program may use at most 192 MiB of HBM per device.

```python
import math
import jax
import jax.numpy as jnp
from jax import lax

DEPTH = 16
NY = 256
FINE = 8
COARSE = 4
CLASSES = 8
SLICES = 32
NX = 128


def touch_ends(entries, rng, smallest, high):
    dims = entries.shape
    place = [jax.random.randint(jax.random.fold_in(rng, axis), (), 0, dims[axis]) for axis in range(len(dims))]
    entries = entries.at[tuple(place)].set(smallest)
    longest = dims.index(max(dims))
    place[longest] = (place[longest] + 1) % dims[longest]
    return entries.at[tuple(place)].set(high)


def shard_levels(stream_key, extent, split, low, high):
    factor_of = 1.0
    for position, parts in split:
        heights = jax.random.uniform(jax.random.fold_in(jax.random.fold_in(stream_key, 6), position), (parts,), jnp.float32, low / len(split), high / len(split))
        factor_of = factor_of * jnp.repeat(jnp.exp(heights), extent[position] // parts).reshape((-1,) + (1,) * (len(extent) - 1 - position))
    return factor_of


def centred(stream_key, dims, width, reach, shards=(), held_as=jnp.bfloat16):
    values = width * jax.random.normal(stream_key, dims, jnp.float32)
    if shards:
        values = values * shard_levels(stream_key, dims, shards, -0.22, 0.18)
    return jnp.clip(values, -reach, reach).astype(held_as)


def setup_inputs(seed: int = 0) -> dict:
    streams_of = jax.random.split(jax.random.key(seed), 8)
    return {
        "starts": centred(streams_of[0], (SLICES, NX, DEPTH, NY), 1.0, 6.0, ((0, 32), (1, 8)), jnp.float32),
        "east_velocity": jnp.clip(jax.random.uniform(streams_of[1], (NX, DEPTH, NY), jnp.float32, -0.3, 0.3) * shard_levels(streams_of[1], (NX, DEPTH, NY), ((0, 8),), -0.4, 0.0), -0.3, 0.3),
        "vertical_velocity": jnp.clip(jax.random.uniform(streams_of[2], (NX, DEPTH, NY), jnp.float32, -0.05, 0.05) * shard_levels(streams_of[2], (NX, DEPTH, NY), ((0, 8),), -0.4, 0.0), -0.05, 0.05),
        "north_velocity": jnp.clip(jax.random.uniform(streams_of[3], (NX, DEPTH, NY), jnp.float32, -0.1, 0.1) * shard_levels(streams_of[3], (NX, DEPTH, NY), ((0, 8),), -0.4, 0.0), -0.1, 0.1),
        "class_map": touch_ends(jax.random.randint(streams_of[4], (NX, DEPTH, NY), 0, CLASSES), jax.random.fold_in(streams_of[4], 1), 0, CLASSES - 1).astype(jnp.int32),
        "land_mask": touch_ends((jax.random.randint(streams_of[5], (NX, DEPTH, NY), 0, 8) < 7).astype(jnp.int32), jax.random.fold_in(streams_of[5], 1), 0, 1),
        "class_diffusivity": jnp.clip(jnp.exp(jax.random.uniform(streams_of[6], (CLASSES,), jnp.float32, math.log(0.005), math.log(0.08))), 0.005, 0.08),
    }


def lower_part(array, direction):
    return lax.slice_in_dim(array, 0, array.shape[direction] - 1, axis=direction)


def upper_part(array, direction):
    return lax.slice_in_dim(array, 1, array.shape[direction], axis=direction)


def advance(tracer, statics, mix_scale):
    diffusivity = statics[3]
    openness = statics[4]
    change = jnp.zeros_like(tracer)
    for direction in range(3):
        speed = statics[direction]
        open_face = lower_part(openness, direction) * upper_part(openness, direction)
        face_speed = 0.5 * (lower_part(speed, direction) + upper_part(speed, direction)) * open_face
        face_mix = mix_scale * 0.5 * (lower_part(diffusivity, direction) + upper_part(diffusivity, direction)) * open_face
        left_value = lower_part(tracer, direction)
        right_value = upper_part(tracer, direction)
        flux = jnp.maximum(face_speed, 0.0) * left_value + jnp.minimum(face_speed, 0.0) * right_value + face_mix * (left_value - right_value)
        pad_widths = [(0, 0), (0, 0), (0, 0)]
        pad_widths[direction] = (1, 1)
        padded_flux = jnp.pad(flux, pad_widths)
        change = change + (upper_part(padded_flux, direction) - lower_part(padded_flux, direction))
    return tracer - change


def restrict(array):
    shape = array.shape
    leading = shape[:-3]
    lead_rank = len(leading)
    reshaped = array.reshape(leading + (shape[-3] // 2, 2, shape[-2] // 2, 2, shape[-1] // 2, 2))
    return jnp.mean(reshaped, axis=(lead_rank + 1, lead_rank + 3, lead_rank + 5))


def prolong(array):
    return jnp.repeat(jnp.repeat(jnp.repeat(array, 2, axis=-3), 2, axis=-2), 2, axis=-1)


def build_statics(east_velocity, vertical_velocity, north_velocity, class_map, land_mask, class_diffusivity):
    classes = jnp.arange(class_diffusivity.shape[0], dtype=jnp.int32)
    diffusivity = jnp.sum(jnp.where(class_map[None] == classes[:, None, None, None], class_diffusivity[:, None, None, None], 0.0), axis=0)
    return jnp.stack([east_velocity, vertical_velocity, north_velocity, diffusivity, land_mask.astype(jnp.float32)])


def reference(starts, east_velocity, vertical_velocity, north_velocity, class_map, land_mask, class_diffusivity):
    statics = build_statics(east_velocity, vertical_velocity, north_velocity, class_map, land_mask, class_diffusivity)
    coarse_statics = restrict(statics)

    def fine_slice(tracer):
        for substep in range(FINE):
            tracer = advance(tracer, statics, 1.0)
        return tracer

    def coarse_prop(tracer):
        for substep in range(COARSE):
            tracer = advance(tracer, coarse_statics, 0.5)
        return tracer

    ends = lax.map(fine_slice, starts)
    own_coarse = restrict(starts)
    first_guess = lax.map(coarse_prop, own_coarse)
    defect = restrict(ends) - first_guess

    def chain_turn(coarse_state, defect_slice):
        latest_one = coarse_prop(coarse_state)
        return latest_one + defect_slice, latest_one

    final_state, latest = lax.scan(chain_turn, own_coarse[0], defect)
    return ends + prolong(latest - first_guess)
```

```python
import functools

import jax
import jax.numpy as jnp
from jax import lax
from jax.experimental import pallas as pl
from jax.experimental.pallas import tpu as pltpu
from jax.sharding import PartitionSpec as P

MESH = pl.DeviceIdType.MESH
W, HF, Z, Y = 16, 4, 16, 256
E = W + 2 * HF
CW, CZ, CY = W // 2, Z // 2, Y // 2
WIN = 5 * CW
TURNS = 4
F32 = jnp.float32


def up(x, axis):
    return pltpu.roll(x, x.shape[axis] - 1, axis)


def down(x, axis):
    return pltpu.roll(x, 1, axis)


def face(speed_a, speed_b, mix_a, mix_b, open_face, scale):
    f = 0.5 * (speed_a + speed_b) * open_face
    h = (0.5 * scale) * (mix_a + mix_b) * open_face
    return jnp.maximum(f, 0.0) + h, h - jnp.minimum(f, 0.0)


def make_coefs(stat, coef, lo, n, scale):
    u, w, v, k, m = stat
    ka, kb = k[lo - 1 : lo + n], k[lo : lo + n + 1]
    ma, mb = m[lo - 1 : lo + n], m[lo : lo + n + 1]
    a, b = face(u[lo - 1 : lo + n], u[lo : lo + n + 1], ka, kb, ma * mb, scale)
    own = slice(lo, lo + n)
    coef[1, own] = a[:n]
    coef[2, own] = b[1:]
    centre = 1.0 - (a[1:] + b[:n])
    kc, mc = kb[:n], mb[:n]
    for axis, field, low, high in ((1, w, 3, 4), (2, v, 5, 6)):
        c = field[own]
        extent = c.shape[axis]
        inside = lax.broadcasted_iota(jnp.int32, c.shape, axis) < extent - 1
        open_face = jnp.where(inside, mc * up(mc, axis), 0.0)
        a, b = face(c, up(c, axis), kc, up(kc, axis), open_face, scale)
        coef[low, own] = down(a, axis)
        coef[high, own] = b
        centre = centre - (a + down(b, axis))
    coef[0, own] = centre


def stencil(coef, q, lo, n):
    own = slice(lo, lo + n)
    c = q[own]
    x = coef[1, own] * q[lo - 1 : lo + n - 1] + coef[2, own] * q[lo + 1 : lo + n + 1]
    z = coef[3, own] * down(c, 1) + coef[4, own] * up(c, 1)
    y = coef[5, own] * down(c, 2) + coef[6, own] * up(c, 2)
    return (coef[0, own] * c + x) + (z + y)


def chunks(lo, hi, size):
    return [(i, min(size, hi - i)) for i in range(lo, hi, size)]


def pick(rows, cols, along):
    r = lax.broadcasted_iota(jnp.int32, (rows, cols), 0)
    c = lax.broadcasted_iota(jnp.int32, (rows, cols), 1)
    return jnp.where((r >> 1) == c if along == 0 else (c >> 1) == r, 1.0, 0.0).astype(F32)


def mul(a, b):
    return jnp.dot(a, b, precision=lax.Precision.HIGHEST, preferred_element_type=F32)


def restrict(pairs):
    flat = pairs.reshape(CW * Z, Y)
    narrow = mul(flat, pick(Y, CY, 0))
    short = mul(pick(CW * CZ, CW * Z, 1), narrow)
    return (0.125 * short).reshape(CW, CZ, CY)


def prolong(coarse):
    flat = mul(coarse.reshape(CW * CZ, CY), pick(CY, Y, 1))
    return mul(pick(CW * Z, CW * CZ, 0), flat).reshape(CW, Z, Y)


def kernel(
    T, S, D0,
    q_in, u_in, w_in, v_in, cls_in, msk_in, kd,
    out,
    st, ints, lv, coef, ends, pairs, s_own, s_next, r_own,
    cs_own, cs_win, ccoef, r_win, e_win, wb, d_out, d_in,
    loc_sem, h_send, h_recv, h2_send, h2_recv, s_sem, r_send, r_recv,
    c_send, c_recv, e_send, e_recv, d_send, d_recv, go,
):
    t, s = lax.axis_index("tm"), lax.axis_index("space")
    K = T // TURNS
    chain = t == D0

    def beside(step):
        return lax.rem(s + step + S, S)

    barrier = pltpu.get_barrier_semaphore()

    def greet(tm, space):
        pl.semaphore_signal(barrier, inc=1, device_id=(tm, space), device_id_type=MESH)

    for step in (-1, 1):
        pl.when((s + step >= 0) & (s + step < S))(functools.partial(greet, t, s + step))
    pl.when(t < T - 1)(lambda: greet(t + 1, s))
    pl.when(t != D0)(lambda: greet(D0, s))

    @pl.when(chain)
    def _():
        for step in (-2, 2):
            pl.when((s + step >= 0) & (s + step < S))(functools.partial(greet, t, s + step))

    fields = ((q_in, lv.at[0]), (u_in, st.at[0]), (w_in, st.at[1]), (v_in, st.at[2]),
              (cls_in, ints.at[0]), (msk_in, ints.at[1]))
    local = [pltpu.make_async_copy(src, dst.at[pl.ds(HF, W)], loc_sem.at[i])
             for i, (src, dst) in enumerate(fields)]
    for copy in local:
        copy.start()

    one = jnp.int32(1)
    zero = jnp.int32(0)

    def flag(condition):
        return jnp.where(condition, one, zero)

    expected = flag(s > 0) + flag(s < S - 1) + flag(t > 0)
    expected = expected + flag(chain) * (T - 1 + flag(s > 1) + flag(s < S - 2))
    pl.semaphore_wait(barrier, expected)

    def halo(i, side):
        src, dst = fields[i]
        src_lo, dst_lo = ((0, HF + W), (W - HF, 0))[side]
        return pltpu.make_async_remote_copy(
            src_ref=src.at[pl.ds(src_lo, HF)], dst_ref=dst.at[pl.ds(dst_lo, HF)],
            send_sem=h_send.at[i, side], recv_sem=h_recv.at[i, side],
            device_id=(t, beside(2 * side - 1)), device_id_type=MESH)

    def halo2(side):
        src_lo, dst_lo = ((HF, HF + W), (W, 0))[side]
        return pltpu.make_async_remote_copy(
            src_ref=lv.at[4, pl.ds(src_lo, HF)], dst_ref=lv.at[4, pl.ds(dst_lo, HF)],
            send_sem=h2_send.at[side], recv_sem=h2_recv.at[side],
            device_id=(t, beside(2 * side - 1)), device_id_type=MESH)

    has_target = (s > 0, s < S - 1)
    order = (1, 2, 3, 4, 5, 0)
    for i in order:
        for side in (0, 1):
            pl.when(has_target[side])(lambda i=i, side=side: halo(i, side).start())

    for has, lo in ((s > 0, 0), (s < S - 1, HF + W)):
        @pl.when(jnp.logical_not(has))
        def _(lo=lo):
            edge = slice(lo, lo + HF)
            blank = jnp.zeros((HF, Z, Y), F32)
            for i in range(3):
                st[i, edge] = blank
            for i in range(2):
                ints[i, edge] = jnp.zeros((HF, Z, Y), jnp.int32)
            lv[0, edge] = blank
            lv[4, edge] = blank

    @pl.when(chain)
    def _():
        def tell(n, carry):
            @pl.when(n != D0)
            def _():
                pl.semaphore_signal(go, inc=1, device_id=(n, s), device_id_type=MESH)
            return carry
        lax.fori_loop(0, T, tell, 0)
        for has, lo in ((s > 1, 0), (s > 0, CW), (s < S - 1, 3 * CW), (s < S - 2, 4 * CW)):
            @pl.when(jnp.logical_not(has))
            def _(lo=lo):
                blank = jnp.zeros((CW, CZ, CY), F32)
                for i in range(5):
                    cs_win[i, lo : lo + CW] = blank

                def clear(n, carry):
                    r_win[n, lo : lo + CW] = blank
                    return carry
                lax.fori_loop(0, T, clear, 0)

                def clear_e(n, carry):
                    e_win[n, lo : lo + CW] = blank
                    return carry
                lax.fori_loop(0, K, clear_e, 0)

    for copy in local:
        copy.wait()

    def widen(lo, n):
        own = slice(lo, lo + n)
        cls = ints[0, own]
        kappa = jnp.zeros(cls.shape, F32)
        for i in range(8):
            kappa = jnp.where(cls == i, kd[i], kappa)
        st[3, own] = kappa
        st[4, own] = ints[1, own].astype(F32)

    def sum_pairs(src, lo):
        for i in range(CW):
            pairs[i] = src[lo + 2 * i] + src[lo + 2 * i + 1]

    sum_pairs(lv.at[0], HF)
    s_own[...] = restrict(pairs[...])
    start_copy = pltpu.make_async_remote_copy(
        src_ref=s_own, dst_ref=s_next, send_sem=s_sem.at[0], recv_sem=s_sem.at[1],
        device_id=(lax.rem(t + T - 1, T), s), device_id_type=MESH)
    pl.when(t > 0)(lambda: start_copy.start())

    stat = [st.at[i] for i in range(5)]
    for lo, n in chunks(HF, HF + W, 2):
        widen(lo, n)
    for lo, n in chunks(HF + 1, HF + W - 1, 2):
        make_coefs(stat, coef, lo, n, 1.0)

    def to_slab(src, dst_of, send, recv, step):
        return pltpu.make_async_remote_copy(
            src_ref=src, dst_ref=dst_of((2 - step) * CW), send_sem=send, recv_sem=recv,
            device_id=(t, beside(step)), device_id_type=MESH)

    steps = (-2, 2, -1, 1)

    def there(step):
        return (s + step >= 0) & (s + step < S)

    def cs_copy(j):
        return to_slab(cs_own, lambda lo: cs_win.at[:, pl.ds(lo, CW)],
                       c_send.at[j], c_recv.at[j], steps[j])

    @pl.when(chain)
    def _():
        for i in range(5):
            sum_pairs(st.at[i], HF)
            part = restrict(pairs[...])
            cs_own[i] = part
            cs_win[i, 2 * CW : 3 * CW] = part
        for j in range(4):
            pl.when(there(steps[j]))(lambda j=j: cs_copy(j).start())

    def fine(src, dst, shift, lo, hi):
        for i, n in chunks(lo, hi, 2):
            dst[i - shift : i - shift + n] = stencil(coef, src, i, n)

    def inner(base):
        for j in range(1, HF + 1):
            last = base + j == 2 * HF
            dst, shift = (ends, HF) if last else (lv.at[base + j], 0)
            fine(lv.at[base + j - 1], dst, shift, HF + j, HF + W - j)

    def outer(base):
        for j in range(1, HF + 1):
            last = base + j == 2 * HF
            dst, shift = (ends, HF) if last else (lv.at[base + j], 0)
            fine(lv.at[base + j - 1], dst, shift, j, HF + j)
            fine(lv.at[base + j - 1], dst, shift, HF + W - j, E - j)

    inner(0)
    for i in order:
        for side in (0, 1):
            pl.when(has_target[1 - side])(lambda i=i, side=side: halo(i, side).wait_recv())
    for lo in (0, HF + W):
        for i, n in chunks(lo, lo + HF, 2):
            widen(i, n)
    for lo in (1, HF + W - 1):
        for i, n in chunks(lo, lo + HF, 2):
            make_coefs(stat, coef, i, n, 1.0)
    outer(0)
    for side in (0, 1):
        pl.when(has_target[side])(lambda side=side: halo2(side).start())
    inner(HF)
    for side in (0, 1):
        pl.when(has_target[1 - side])(lambda side=side: halo2(side).wait_recv())
    outer(HF)

    sum_pairs(ends, 0)
    pl.when(t < T - 1)(lambda: start_copy.wait_recv())
    pl.when(t != D0)(lambda: pl.semaphore_wait(go, 1))

    def r_copy(n, kind, j):
        step = (0,) + steps
        step = step[j]
        size = CW if step == 0 or (abs(step) == 1 and kind < 2) else CW // 2
        lo = CW - size if step > 0 else 0
        return pltpu.make_async_remote_copy(
            src_ref=r_own.at[pl.ds(lo, size)],
            dst_ref=r_win.at[n, pl.ds((2 - step) * CW + lo, size)],
            send_sem=r_send.at[j], recv_sem=r_recv.at[n, j],
            device_id=(D0, beside(step)), device_id_type=MESH)

    pieces = ((0, 1, 2, 3, 4), (0, 3, 4), (0, 3, 4), (0,))

    def r_each(n, act, wait):
        for kind in range(TURNS):
            @pl.when(lax.rem(n, TURNS) == kind)
            def _(kind=kind):
                r_pieces(n, kind, act, wait)

    def r_pieces(n, kind, act, wait):
        for j in pieces[kind]:
            step = ((0,) + steps)[j]
            condition = (n != D0) if step == 0 else there(-step if wait else step)
            pl.when(condition)(lambda j=j: act(r_copy(n, kind, j)))

    @pl.when(t < T - 1)
    def _():
        r_own[...] = restrict(pairs[...]) - s_next[...]

        @pl.when(chain)
        def _():
            r_win[D0, 2 * CW : 3 * CW] = r_own[...]
        r_each(t, lambda copy: copy.start(), False)

    def d_copy(n):
        return pltpu.make_async_remote_copy(
            src_ref=d_out.at[n], dst_ref=d_in, send_sem=d_send.at[n], recv_sem=d_recv,
            device_id=(n, s), device_id_type=MESH)

    def e_copy(k, j):
        return to_slab(e_win.at[k, pl.ds(2 * CW, CW)], lambda lo: e_win.at[k, pl.ds(lo, CW)],
                       e_send.at[k, j], e_recv.at[k, j], steps[j])

    def turn(n, kind, src, dst, last):
        lo, hi = 4 * kind, WIN - 4 * kind
        for j in range(1, 4):
            for i, m in chunks(lo + j, hi - j, CW):
                wb[1 - j % 2, i : i + m] = stencil(ccoef, src, i, m)
            src = wb.at[1 - j % 2]
        if not last:
            r_pieces(n, kind, lambda copy: copy.wait_recv(), True)
        own_lo, own_hi = 2 * CW, 3 * CW
        parts = chunks(lo + 4, own_lo, CW) + [(own_lo, CW)] + chunks(own_hi, hi - 4, CW)
        for i, m in parts:
            fresh = stencil(ccoef, src, i, m)
            if i != own_lo:
                dst[i : i + m] = fresh + r_win[n, i : i + m]
                continue
            d_out[n] = fresh
            if not last:
                dst[i : i + m] = fresh + r_win[n, i : i + m]

        @pl.when(n != D0)
        def _():
            d_copy(n).start()

        @pl.when(n == D0)
        def _():
            d_in[...] = d_out[n]

    @pl.when(chain)
    def _():
        for j in range(4):
            pl.when(there(-steps[j]))(lambda j=j: cs_copy(j).wait_recv())
        cstat = [cs_win.at[i] for i in range(5)]
        for lo, n in chunks(1, WIN - 1, 4):
            make_coefs(cstat, ccoef, lo, n, 0.5)

        r_pieces(0, 0, lambda copy: copy.wait_recv(), True)
        src = r_win.at[0]
        for kind in range(1, TURNS):
            dst = wb.at[1] if kind < TURNS - 1 else e_win.at[1]
            turn(kind, kind, src, dst, False)
            src = wb.at[1]

        def cycle(k, final):
            for j in range(4):
                pl.when(there(steps[j]))(lambda j=j: e_copy(k, j).start())
            for j in range(4):
                pl.when(there(-steps[j]))(lambda j=j: e_copy(k, j).wait_recv())
            src = e_win.at[k]
            for kind in range(TURNS):
                last = kind == TURNS - 1
                dst = (None if final else e_win.at[k + 1]) if last else wb.at[1]
                turn(TURNS * k + kind, kind, src, dst, final and last)
                src = wb.at[1]

        def body(k, carry):
            cycle(k, False)
            return carry
        lax.fori_loop(1, K - 1, body, 0)
        cycle(K - 1, True)

    pl.when((t > 0) & (t != D0))(lambda: d_copy(t).wait_recv())

    @pl.when(t == 0)
    def _():
        out[...] = ends[...]

    @pl.when(t > 0)
    def _():
        fine_delta = prolong(d_in[...])
        for i in range(CW):
            out[2 * i] = ends[2 * i] + fine_delta[i]
            out[2 * i + 1] = ends[2 * i + 1] + fine_delta[i]

    for side in (0, 1):
        for i in order:
            pl.when(has_target[side])(lambda i=i, side=side: halo(i, side).wait_send())
        pl.when(has_target[side])(lambda side=side: halo2(side).wait_send())
    pl.when(t > 0)(lambda: start_copy.wait_send())
    pl.when(t < T - 1)(lambda: r_each(t, lambda copy: copy.wait_send(), False))

    @pl.when(chain)
    def _():
        for j in range(4):
            pl.when(there(steps[j]))(lambda j=j: cs_copy(j).wait_send())

        def drain_e(k, carry):
            for j in range(4):
                pl.when(there(steps[j]))(lambda j=j: e_copy(k, j).wait_send())
            return carry
        lax.fori_loop(1, K, drain_e, 0)

        def drain_d(n, carry):
            pl.when(n != D0)(lambda: d_copy(n).wait_send())
            return carry
        lax.fori_loop(1, T, drain_d, 0)


def shards(starts, u, w, v, cls, msk, kd):
    T, S = lax.axis_size("tm"), lax.axis_size("space")
    K = T // TURNS
    D0 = (3 * T) // 4
    dma = pltpu.SemaphoreType.DMA
    anywhere = pl.BlockSpec(memory_space=pl.ANY)
    slab = (CW, CZ, CY)
    result = pl.pallas_call(
        functools.partial(kernel, T, S, D0),
        out_shape=jax.ShapeDtypeStruct((W, Z, Y), F32),
        in_specs=[anywhere] * 6 + [pl.BlockSpec(memory_space=pltpu.SMEM)],
        out_specs=pl.BlockSpec(memory_space=pltpu.VMEM),
        scratch_shapes=[
            pltpu.VMEM((5, E, Z, Y), F32),
            pltpu.VMEM((2, E, Z, Y), jnp.int32),
            pltpu.VMEM((8, E, Z, Y), F32),
            pltpu.VMEM((7, E, Z, Y), F32),
            pltpu.VMEM((W, Z, Y), F32),
            pltpu.VMEM((CW, Z, Y), F32),
            pltpu.VMEM(slab, F32),
            pltpu.VMEM(slab, F32),
            pltpu.VMEM(slab, F32),
            pltpu.VMEM((5,) + slab, F32),
            pltpu.VMEM((5, WIN, CZ, CY), F32),
            pltpu.VMEM((7, WIN, CZ, CY), F32),
            pltpu.VMEM((T, WIN, CZ, CY), F32),
            pltpu.VMEM((K, WIN, CZ, CY), F32),
            pltpu.VMEM((2, WIN, CZ, CY), F32),
            pltpu.VMEM((T,) + slab, F32),
            pltpu.VMEM(slab, F32),
            dma((6,)),
            dma((6, 2)), dma((6, 2)),
            dma((2,)), dma((2,)),
            dma((2,)),
            dma((5,)), dma((T, 5)),
            dma((4,)), dma((4,)),
            dma((K, 4)), dma((K, 4)),
            dma((T,)), dma(()),
            pltpu.SemaphoreType.REGULAR,
        ],
        compiler_params=pltpu.CompilerParams(
            collective_id=0, has_side_effects=True, vmem_limit_bytes=56 * 1024 * 1024),
    )(starts[0], u, w, v, cls, msk, kd)
    return result[None]


def solution(mesh):
    slabs = P("space", None, None)
    return jax.shard_map(
        shards, mesh=mesh,
        in_specs=(P("tm", "space", None, None),) + (slabs,) * 5 + (P(),),
        out_specs=P("tm", "space", None, None), check_vma=False)
```

```python
import functools

import jax
import jax.numpy as jnp
from jax import lax
from jax.experimental import pallas as pl
from jax.experimental.pallas import tpu as pltpu
from jax.sharding import PartitionSpec as P

MESH = pl.DeviceIdType.MESH
W, HF, Z, Y = 16, 4, 16, 256
E = W + 2 * HF
CW, CZ, CY = W // 2, Z // 2, Y // 2
WIN = 5 * CW
TURNS = 4
GROUP = 2 * TURNS
F32 = jnp.float32


def up(x, axis):
    return pltpu.roll(x, x.shape[axis] - 1, axis)


def down(x, axis):
    return pltpu.roll(x, 1, axis)


def face(speed_a, speed_b, mix_a, mix_b, open_face, scale):
    f = 0.5 * (speed_a + speed_b) * open_face
    h = (0.5 * scale) * (mix_a + mix_b) * open_face
    return jnp.maximum(f, 0.0) + h, h - jnp.minimum(f, 0.0)


def make_coefs(stat, coef, lo, n, scale):
    u, w, v, k, m = stat
    ka, kb = k[lo - 1 : lo + n], k[lo : lo + n + 1]
    ma, mb = m[lo - 1 : lo + n], m[lo : lo + n + 1]
    a, b = face(u[lo - 1 : lo + n], u[lo : lo + n + 1], ka, kb, ma * mb, scale)
    own = slice(lo, lo + n)
    coef[1, own] = a[:n]
    coef[2, own] = b[1:]
    centre = 1.0 - (a[1:] + b[:n])
    kc, mc = kb[:n], mb[:n]
    for axis, field, low, high in ((1, w, 3, 4), (2, v, 5, 6)):
        c = field[own]
        extent = c.shape[axis]
        inside = lax.broadcasted_iota(jnp.int32, c.shape, axis) < extent - 1
        open_face = jnp.where(inside, mc * up(mc, axis), 0.0)
        a, b = face(c, up(c, axis), kc, up(kc, axis), open_face, scale)
        coef[low, own] = down(a, axis)
        coef[high, own] = b
        centre = centre - (a + down(b, axis))
    coef[0, own] = centre


def stencil(coef, q, lo, n):
    own = slice(lo, lo + n)
    c = q[own]
    x = coef[1, own] * q[lo - 1 : lo + n - 1] + coef[2, own] * q[lo + 1 : lo + n + 1]
    z = coef[3, own] * down(c, 1) + coef[4, own] * up(c, 1)
    y = coef[5, own] * down(c, 2) + coef[6, own] * up(c, 2)
    return (coef[0, own] * c + x) + (z + y)


def chunks(lo, hi, size):
    return [(i, min(size, hi - i)) for i in range(lo, hi, size)]


def pick(rows, cols, along):
    r = lax.broadcasted_iota(jnp.int32, (rows, cols), 0)
    c = lax.broadcasted_iota(jnp.int32, (rows, cols), 1)
    return jnp.where((r >> 1) == c if along == 0 else (c >> 1) == r, 1.0, 0.0).astype(F32)


def mul(a, b):
    return jnp.dot(a, b, precision=lax.Precision.HIGHEST, preferred_element_type=F32)


def restrict(pairs):
    flat = pairs.reshape(CW * Z, Y)
    narrow = mul(flat, pick(Y, CY, 0))
    short = mul(pick(CW * CZ, CW * Z, 1), narrow)
    return (0.125 * short).reshape(CW, CZ, CY)


def prolong(coarse):
    flat = mul(coarse.reshape(CW * CZ, CY), pick(CY, Y, 1))
    return mul(pick(CW * Z, CW * CZ, 0), flat).reshape(CW, Z, Y)


def kernel(
    T, S,
    q_in, u_in, w_in, v_in, cls_in, msk_in, kd,
    out,
    st, ints, lv, coef, ends, pairs, s_own, s_next, r_own,
    cs_own, cs_win, ccoef, r_win, e_win, wb, d_out, d_in,
    cs_full, fcoef, p_own, p_full, cur, g_out, g_in,
    loc_sem, h_send, h_recv, h2_send, h2_recv, s_sem, r_send, r_recv,
    c_send, c_recv, e_send, e_recv, d_send, d_recv,
    f_send, f_recv, p_send, p_recv, g_send, g_recv, go,
):
    t, s = lax.axis_index("tm"), lax.axis_index("space")
    groups = T // GROUP
    MAIN = T - GROUP
    slot = lax.rem(t, GROUP)
    home = t - slot
    chain = slot == 0
    main = t == MAIN

    def beside(step):
        return lax.rem(s + step + S, S)

    barrier = pltpu.get_barrier_semaphore()

    def greet(tm, space):
        pl.semaphore_signal(barrier, inc=1, device_id=(tm, space), device_id_type=MESH)

    for step in (-1, 1):
        pl.when((s + step >= 0) & (s + step < S))(functools.partial(greet, t, s + step))
    pl.when(t < T - 1)(lambda: greet(t + 1, s))
    pl.when(slot != 0)(lambda: greet(home, s))
    pl.when((t >= GROUP) & (t != MAIN))(lambda: greet(MAIN, s))

    @pl.when(chain)
    def _():
        for step in (-2, 2):
            pl.when((s + step >= 0) & (s + step < S))(functools.partial(greet, t, s + step))

    @pl.when(main)
    def _():
        for z in range(S):
            for x in range(groups - 1):
                greet(x * GROUP, z)
            pl.when(s != z)(functools.partial(greet, t, z))

    fields = ((q_in, lv.at[0]), (u_in, st.at[0]), (w_in, st.at[1]), (v_in, st.at[2]),
              (cls_in, ints.at[0]), (msk_in, ints.at[1]))
    local = [pltpu.make_async_copy(src, dst.at[pl.ds(HF, W)], loc_sem.at[i])
             for i, (src, dst) in enumerate(fields)]
    for copy in local:
        copy.start()

    one = jnp.int32(1)
    zero = jnp.int32(0)

    def flag(condition):
        return jnp.where(condition, one, zero)

    expected = flag(s > 0) + flag(s < S - 1) + flag(t > 0)
    expected = expected + flag(chain) * (GROUP - 1 + flag(s > 1) + flag(s < S - 2))
    expected = expected + flag(chain & (t != MAIN)) * S + flag(main) * (T - GROUP - 1 + S - 1)
    pl.semaphore_wait(barrier, expected)

    def halo(i, side):
        src, dst = fields[i]
        src_lo, dst_lo = ((0, HF + W), (W - HF, 0))[side]
        return pltpu.make_async_remote_copy(
            src_ref=src.at[pl.ds(src_lo, HF)], dst_ref=dst.at[pl.ds(dst_lo, HF)],
            send_sem=h_send.at[i, side], recv_sem=h_recv.at[i, side],
            device_id=(t, beside(2 * side - 1)), device_id_type=MESH)

    def halo2(side):
        src_lo, dst_lo = ((HF, HF + W), (W, 0))[side]
        return pltpu.make_async_remote_copy(
            src_ref=lv.at[4, pl.ds(src_lo, HF)], dst_ref=lv.at[4, pl.ds(dst_lo, HF)],
            send_sem=h2_send.at[side], recv_sem=h2_recv.at[side],
            device_id=(t, beside(2 * side - 1)), device_id_type=MESH)

    has_target = (s > 0, s < S - 1)
    order = (1, 2, 3, 4, 5, 0)
    for i in order:
        for side in (0, 1):
            pl.when(has_target[side])(lambda i=i, side=side: halo(i, side).start())

    for has, lo in ((s > 0, 0), (s < S - 1, HF + W)):
        @pl.when(jnp.logical_not(has))
        def _(lo=lo):
            edge = slice(lo, lo + HF)
            blank = jnp.zeros((HF, Z, Y), F32)
            for i in range(3):
                st[i, edge] = blank
            for i in range(2):
                ints[i, edge] = jnp.zeros((HF, Z, Y), jnp.int32)
            lv[0, edge] = blank
            lv[4, edge] = blank

    @pl.when(chain)
    def _():
        for n in range(1, GROUP):
            pl.semaphore_signal(go, inc=1, device_id=(home + n, s), device_id_type=MESH)
        for has, lo in ((s > 1, 0), (s > 0, CW), (s < S - 1, 3 * CW), (s < S - 2, 4 * CW)):
            @pl.when(jnp.logical_not(has))
            def _(lo=lo):
                blank = jnp.zeros((CW, CZ, CY), F32)
                for i in range(5):
                    cs_win[i, lo : lo + CW] = blank

                for n in range(GROUP):
                    r_win[n, lo : lo + CW] = blank
                e_win[lo : lo + CW] = blank

    @pl.when(main)
    def _():
        margin = jnp.zeros((1, CZ, CY), F32)
        for lo in (0, S * CW + 1):
            for i in range(5):
                cs_full[i, lo : lo + 1] = margin
            for i in range(3):
                cur[i, lo : lo + 1] = margin
        for i in range(S):
            cur[0, 1 + i * CW : 1 + (i + 1) * CW] = jnp.zeros((CW, CZ, CY), F32)

    for copy in local:
        copy.wait()

    def widen(lo, n):
        own = slice(lo, lo + n)
        cls = ints[0, own]
        kappa = jnp.zeros(cls.shape, F32)
        for i in range(8):
            kappa = jnp.where(cls == i, kd[i], kappa)
        st[3, own] = kappa
        st[4, own] = ints[1, own].astype(F32)

    def sum_pairs(src, lo):
        for i in range(CW):
            pairs[i] = src[lo + 2 * i] + src[lo + 2 * i + 1]

    sum_pairs(lv.at[0], HF)
    s_own[...] = restrict(pairs[...])
    start_copy = pltpu.make_async_remote_copy(
        src_ref=s_own, dst_ref=s_next, send_sem=s_sem.at[0], recv_sem=s_sem.at[1],
        device_id=(lax.rem(t + T - 1, T), s), device_id_type=MESH)
    pl.when(t > 0)(lambda: start_copy.start())

    stat = [st.at[i] for i in range(5)]
    for lo, n in chunks(HF, HF + W, 2):
        widen(lo, n)
    for lo, n in chunks(HF + 1, HF + W - 1, 2):
        make_coefs(stat, coef, lo, n, 1.0)

    def to_slab(src, dst_of, send, recv, step):
        return pltpu.make_async_remote_copy(
            src_ref=src, dst_ref=dst_of((2 - step) * CW), send_sem=send, recv_sem=recv,
            device_id=(t, beside(step)), device_id_type=MESH)

    steps = (-2, 2, -1, 1)

    def there(step):
        return (s + step >= 0) & (s + step < S)

    def cs_copy(j):
        return to_slab(cs_own, lambda lo: cs_win.at[:, pl.ds(lo, CW)],
                       c_send.at[j], c_recv.at[j], steps[j])

    @pl.when(chain)
    def _():
        for i in range(5):
            sum_pairs(st.at[i], HF)
            part = restrict(pairs[...])
            cs_own[i] = part
            cs_win[i, 2 * CW : 3 * CW] = part
        for j in range(4):
            pl.when(there(steps[j]))(lambda j=j: cs_copy(j).start())

    def f_copy(z):
        return pltpu.make_async_remote_copy(
            src_ref=cs_own, dst_ref=cs_full.at[:, pl.ds(1 + s * CW, CW)],
            send_sem=f_send.at[z], recv_sem=f_recv.at[s],
            device_id=(MAIN, z), device_id_type=MESH)

    def f_arrival(z):
        return pltpu.make_async_remote_copy(
            src_ref=cs_own, dst_ref=cs_full.at[:, pl.ds(1 + z * CW, CW)],
            send_sem=f_send.at[z], recv_sem=f_recv.at[z],
            device_id=(MAIN, z), device_id_type=MESH)

    @pl.when(main)
    def _():
        cs_full[:, pl.ds(1 + s * CW, CW)] = cs_own[...]

    def fine(src, dst, shift, lo, hi):
        for i, n in chunks(lo, hi, 2):
            dst[i - shift : i - shift + n] = stencil(coef, src, i, n)

    def inner(base):
        for j in range(1, HF + 1):
            last = base + j == 2 * HF
            dst, shift = (ends, HF) if last else (lv.at[base + j], 0)
            fine(lv.at[base + j - 1], dst, shift, HF + j, HF + W - j)

    def outer(base):
        for j in range(1, HF + 1):
            last = base + j == 2 * HF
            dst, shift = (ends, HF) if last else (lv.at[base + j], 0)
            fine(lv.at[base + j - 1], dst, shift, j, HF + j)
            fine(lv.at[base + j - 1], dst, shift, HF + W - j, E - j)

    inner(0)
    for i in order:
        for side in (0, 1):
            pl.when(has_target[1 - side])(lambda i=i, side=side: halo(i, side).wait_recv())
    for lo in (0, HF + W):
        for i, n in chunks(lo, lo + HF, 2):
            widen(i, n)
    for lo in (1, HF + W - 1):
        for i, n in chunks(lo, lo + HF, 2):
            make_coefs(stat, coef, i, n, 1.0)
    outer(0)
    for side in (0, 1):
        pl.when(has_target[side])(lambda side=side: halo2(side).start())

    @pl.when(main)
    def _():
        for z in range(S):
            pl.when(s != z)(lambda z=z: f_copy(z).start())

    inner(HF)
    for side in (0, 1):
        pl.when(has_target[1 - side])(lambda side=side: halo2(side).wait_recv())
    outer(HF)

    sum_pairs(ends, 0)
    pl.when(t < T - 1)(lambda: start_copy.wait_recv())
    pl.when(slot != 0)(lambda: pl.semaphore_wait(go, 1))

    def r_copy(n, kind, j):
        step = (0,) + steps
        step = step[j]
        size = CW if step == 0 or (abs(step) == 1 and kind < 2) else CW // 2
        lo = CW - size if step > 0 else 0
        return pltpu.make_async_remote_copy(
            src_ref=r_own.at[pl.ds(lo, size)],
            dst_ref=r_win.at[n, pl.ds((2 - step) * CW + lo, size)],
            send_sem=r_send.at[j], recv_sem=r_recv.at[n, j],
            device_id=(home, beside(step)), device_id_type=MESH)

    pieces = ((0, 1, 2, 3, 4), (0, 3, 4), (0, 3, 4), (0,))

    def r_each(n, act, wait):
        for kind in range(TURNS):
            @pl.when(lax.rem(n, TURNS) == kind)
            def _(kind=kind):
                r_pieces(n, kind, act, wait)

    def r_pieces(n, kind, act, wait):
        for j in pieces[kind]:
            step = ((0,) + steps)[j]
            own_slab = n != 0
            condition = own_slab if step == 0 else there(-step if wait else step)
            if condition is True:
                act(r_copy(n, kind, j))
            elif condition is not False:
                pl.when(condition)(lambda j=j: act(r_copy(n, kind, j)))

    @pl.when(t < T - 1)
    def _():
        r_own[...] = restrict(pairs[...]) - s_next[...]

        @pl.when(chain)
        def _():
            r_win[0, 2 * CW : 3 * CW] = r_own[...]
        r_each(slot, lambda copy: copy.start(), False)

    def d_copy(n):
        return pltpu.make_async_remote_copy(
            src_ref=d_out.at[n], dst_ref=d_in, send_sem=d_send.at[n], recv_sem=d_recv,
            device_id=(home + n, s), device_id_type=MESH)

    def e_copy(j):
        return to_slab(e_win.at[pl.ds(2 * CW, CW)], lambda lo: e_win.at[pl.ds(lo, CW)],
                       e_send.at[j], e_recv.at[j], steps[j])

    def p_copy(z):
        return pltpu.make_async_remote_copy(
            src_ref=p_own, dst_ref=p_full.at[home // GROUP, pl.ds(s * CW, CW)],
            send_sem=p_send.at[z], recv_sem=p_recv.at[home // GROUP, s],
            device_id=(MAIN, z), device_id_type=MESH)

    def p_arrival(x, z):
        return pltpu.make_async_remote_copy(
            src_ref=p_own, dst_ref=p_full.at[x, pl.ds(z * CW, CW)],
            send_sem=p_send.at[z], recv_sem=p_recv.at[x, z],
            device_id=(MAIN, z), device_id_type=MESH)

    def turn(n, src, dst):
        kind = n % TURNS
        lo, hi = 4 * kind, WIN - 4 * kind
        for j in range(1, 4):
            for i, m in chunks(lo + j, hi - j, CW):
                wb[1 - j % 2, i : i + m] = stencil(ccoef, src, i, m)
            src = wb.at[1 - j % 2]
        own_lo, own_hi = 2 * CW, 3 * CW
        d_out[n] = stencil(ccoef, src, own_lo, CW)
        d_copy(n).start()

        if n == GROUP - 1:
            @pl.when(t != MAIN)
            def _():
                r_pieces(n, kind, lambda copy: copy.wait_recv(), True)
                p_own[...] = d_out[n] + r_win[n, own_lo:own_hi]
                for z in range(S):
                    p_copy(z).start()
            return
        r_pieces(n, kind, lambda copy: copy.wait_recv(), True)
        into = slice(own_lo, own_hi)
        dst[into] = d_out[n] + r_win[n, into]
        for i, m in chunks(lo + 4, own_lo, CW) + chunks(own_hi, hi - 4, CW):
            dst[i : i + m] = stencil(ccoef, src, i, m) + r_win[n, i : i + m]

    @pl.when(chain)
    def _():
        for j in range(4):
            pl.when(there(-steps[j]))(lambda j=j: cs_copy(j).wait_recv())
        cstat = [cs_win.at[i] for i in range(5)]
        for lo, n in chunks(1, WIN - 1, 4):
            make_coefs(cstat, ccoef, lo, n, 0.5)

        r_pieces(0, 0, lambda copy: copy.wait_recv(), True)
        src = r_win.at[0]
        for n in range(1, TURNS):
            turn(n, src, wb.at[1] if n < TURNS - 1 else e_win)
            src = wb.at[1]
        for j in range(4):
            pl.when(there(steps[j]))(lambda j=j: e_copy(j).start())
        for j in range(4):
            pl.when(there(-steps[j]))(lambda j=j: e_copy(j).wait_recv())
        src = e_win
        for n in range(TURNS, GROUP):
            turn(n, src, wb.at[1])
            src = wb.at[1]

    def g_copy(m):
        return pltpu.make_async_remote_copy(
            src_ref=g_out.at[m], dst_ref=g_in, send_sem=g_send.at[m], recv_sem=g_recv,
            device_id=(m + GROUP, s), device_id_type=MESH)

    @pl.when(main)
    def _():
        for z in range(S):
            pl.when(s != z)(lambda z=z: f_arrival(z).wait_recv())
        fstat = [cs_full.at[i] for i in range(5)]
        for lo, n in chunks(1, S * CW + 1, 4):
            make_coefs(fstat, fcoef, lo, n, 0.5)

        def big_turn(m, carry):
            @pl.when(lax.rem(m, GROUP) == 0)
            def _():
                x = m // GROUP
                for z in range(S):
                    p_arrival(x, z).wait_recv()
                for i, n in chunks(0, S * CW, CW):
                    cur[0, i + 1 : i + 1 + n] = cur[0, i + 1 : i + 1 + n] + p_full[x, i : i + n]

            for a, b in ((0, 1), (1, 2), (2, 1), (1, 0)):
                for i, n in chunks(1, S * CW + 1, CW):
                    cur[b, i : i + n] = stencil(fcoef, cur.at[a], i, n)
            g_out[m] = cur[0, pl.ds(1 + s * CW, CW)]
            pl.when(m + GROUP != MAIN)(lambda: g_copy(m).start())
            return carry
        lax.fori_loop(0, T - GROUP, big_turn, 0)

    pl.when(slot > 0)(lambda: d_copy(slot).wait_recv())
    pl.when((t >= GROUP) & (t != MAIN))(lambda: g_copy(t - GROUP).wait_recv())

    @pl.when(main)
    def _():
        g_in[...] = g_out[MAIN - GROUP]

    @pl.when(slot == 0)
    def _():
        d_in[...] = jnp.zeros((CW, CZ, CY), F32)

    @pl.when(t >= GROUP)
    def _():
        d_in[...] = d_in[...] + g_in[...]

    fine_delta = prolong(d_in[...])
    for i in range(CW):
        out[2 * i] = ends[2 * i] + fine_delta[i]
        out[2 * i + 1] = ends[2 * i + 1] + fine_delta[i]

    for side in (0, 1):
        for i in order:
            pl.when(has_target[side])(lambda i=i, side=side: halo(i, side).wait_send())
        pl.when(has_target[side])(lambda side=side: halo2(side).wait_send())
    pl.when(t > 0)(lambda: start_copy.wait_send())
    pl.when(t < T - 1)(lambda: r_each(slot, lambda copy: copy.wait_send(), False))

    @pl.when(chain)
    def _():
        for j in range(4):
            pl.when(there(steps[j]))(lambda j=j: cs_copy(j).wait_send())

            pl.when(there(steps[j]))(lambda j=j: e_copy(j).wait_send())
        for n in range(1, GROUP):
            d_copy(n).wait_send()

        @pl.when(t != MAIN)
        def _():
            for z in range(S):
                p_copy(z).wait_send()

    @pl.when(main)
    def _():
        for z in range(S):
            pl.when(s != z)(lambda z=z: f_copy(z).wait_send())

        def drain(m, carry):
            pl.when(m + GROUP != MAIN)(lambda: g_copy(m).wait_send())
            return carry
        lax.fori_loop(0, T - GROUP, drain, 0)


def shards(starts, u, w, v, cls, msk, kd):
    T, S = lax.axis_size("tm"), lax.axis_size("space")
    groups = T // GROUP
    dma = pltpu.SemaphoreType.DMA
    anywhere = pl.BlockSpec(memory_space=pl.ANY)
    slab = (CW, CZ, CY)
    result = pl.pallas_call(
        functools.partial(kernel, T, S),
        out_shape=jax.ShapeDtypeStruct((W, Z, Y), F32),
        in_specs=[anywhere] * 6 + [pl.BlockSpec(memory_space=pltpu.SMEM)],
        out_specs=pl.BlockSpec(memory_space=pltpu.VMEM),
        scratch_shapes=[
            pltpu.VMEM((5, E, Z, Y), F32),
            pltpu.VMEM((2, E, Z, Y), jnp.int32),
            pltpu.VMEM((8, E, Z, Y), F32),
            pltpu.VMEM((7, E, Z, Y), F32),
            pltpu.VMEM((W, Z, Y), F32),
            pltpu.VMEM((CW, Z, Y), F32),
            pltpu.VMEM(slab, F32),
            pltpu.VMEM(slab, F32),
            pltpu.VMEM(slab, F32),
            pltpu.VMEM((5,) + slab, F32),
            pltpu.VMEM((5, WIN, CZ, CY), F32),
            pltpu.VMEM((7, WIN, CZ, CY), F32),
            pltpu.VMEM((GROUP, WIN, CZ, CY), F32),
            pltpu.VMEM((WIN, CZ, CY), F32),
            pltpu.VMEM((2, WIN, CZ, CY), F32),
            pltpu.VMEM((GROUP,) + slab, F32),
            pltpu.VMEM(slab, F32),
            pltpu.VMEM((5, S * CW + 2, CZ, CY), F32),
            pltpu.VMEM((7, S * CW + 2, CZ, CY), F32),
            pltpu.VMEM(slab, F32),
            pltpu.VMEM((groups - 1, S * CW, CZ, CY), F32),
            pltpu.VMEM((3, S * CW + 2, CZ, CY), F32),
            pltpu.VMEM((T - GROUP,) + slab, F32),
            pltpu.VMEM(slab, F32),
            dma((6,)),
            dma((6, 2)), dma((6, 2)),
            dma((2,)), dma((2,)),
            dma((2,)),
            dma((5,)), dma((GROUP, 5)),
            dma((4,)), dma((4,)),
            dma((4,)), dma((4,)),
            dma((GROUP,)), dma(()),
            dma((S,)), dma((S,)),
            dma((S,)), dma((groups - 1, S)),
            dma((T - GROUP,)), dma(()),
            pltpu.SemaphoreType.REGULAR,
        ],
        compiler_params=pltpu.CompilerParams(
            collective_id=0, has_side_effects=True, vmem_limit_bytes=56 * 1024 * 1024),
    )(starts[0], u, w, v, cls, msk, kd)
    return result[None]


def solution(mesh):
    slabs = P("space", None, None)
    return jax.shard_map(
        shards, mesh=mesh,
        in_specs=(P("tm", "space", None, None),) + (slabs,) * 5 + (P(),),
        out_specs=P("tm", "space", None, None), check_vma=False)
```

```python
import functools

import jax
import jax.numpy as jnp
from jax import lax
from jax.experimental import pallas as pl
from jax.experimental.pallas import tpu as pltpu
from jax.sharding import PartitionSpec as P

MESH = pl.DeviceIdType.MESH
W, HF, Z, Y = 16, 4, 16, 256
E = W + 2 * HF
CW, CZ, CY = W // 2, Z // 2, Y // 2
WIN = 5 * CW
TURNS = 4
GROUP = 2 * TURNS
F32 = jnp.float32


def up(x, axis):
    return pltpu.roll(x, x.shape[axis] - 1, axis)


def down(x, axis):
    return pltpu.roll(x, 1, axis)


def face(speed_a, speed_b, mix_a, mix_b, open_face, scale):
    f = 0.5 * (speed_a + speed_b) * open_face
    h = (0.5 * scale) * (mix_a + mix_b) * open_face
    return jnp.maximum(f, 0.0) + h, h - jnp.minimum(f, 0.0)


def make_coefs(stat, coef, lo, n, scale):
    u, w, v, k, m = stat
    ka, kb = k[lo - 1 : lo + n], k[lo : lo + n + 1]
    ma, mb = m[lo - 1 : lo + n], m[lo : lo + n + 1]
    a, b = face(u[lo - 1 : lo + n], u[lo : lo + n + 1], ka, kb, ma * mb, scale)
    own = slice(lo, lo + n)
    coef[1, own] = a[:n]
    coef[2, own] = b[1:]
    centre = 1.0 - (a[1:] + b[:n])
    kc, mc = kb[:n], mb[:n]
    for axis, field, low, high in ((1, w, 3, 4), (2, v, 5, 6)):
        c = field[own]
        extent = c.shape[axis]
        inside = lax.broadcasted_iota(jnp.int32, c.shape, axis) < extent - 1
        open_face = jnp.where(inside, mc * up(mc, axis), 0.0)
        a, b = face(c, up(c, axis), kc, up(kc, axis), open_face, scale)
        coef[low, own] = down(a, axis)
        coef[high, own] = b
        centre = centre - (a + down(b, axis))
    coef[0, own] = centre


def stencil(coef, q, lo, n):
    own = slice(lo, lo + n)
    c = q[own]
    x = coef[1, own] * q[lo - 1 : lo + n - 1] + coef[2, own] * q[lo + 1 : lo + n + 1]
    z = coef[3, own] * down(c, 1) + coef[4, own] * up(c, 1)
    y = coef[5, own] * down(c, 2) + coef[6, own] * up(c, 2)
    return (coef[0, own] * c + x) + (z + y)


def chunks(lo, hi, size):
    return [(i, min(size, hi - i)) for i in range(lo, hi, size)]


def pick(rows, cols, along):
    r = lax.broadcasted_iota(jnp.int32, (rows, cols), 0)
    c = lax.broadcasted_iota(jnp.int32, (rows, cols), 1)
    return jnp.where((r >> 1) == c if along == 0 else (c >> 1) == r, 1.0, 0.0).astype(F32)


def mul(a, b):
    return jnp.dot(a, b, precision=lax.Precision.HIGHEST, preferred_element_type=F32)


def restrict(pairs):
    flat = pairs.reshape(CW * Z, Y)
    narrow = mul(flat, pick(Y, CY, 0))
    short = mul(pick(CW * CZ, CW * Z, 1), narrow)
    return (0.125 * short).reshape(CW, CZ, CY)


def prolong(coarse):
    flat = mul(coarse.reshape(CW * CZ, CY), pick(CY, Y, 1))
    return mul(pick(CW * Z, CW * CZ, 0), flat).reshape(CW, Z, Y)


def kernel(
    T, S,
    q_in, u_in, w_in, v_in, cls_in, msk_in, kd,
    out,
    st, ints, lv, coef, ends, pairs, s_own, s_next, r_own,
    cs_own, cs_win, ccoef, r_win, e_win, wb, d_out, d_in,
    cs_full, fcoef, p_own, p_full, cur, g_out, g_in,
    loc_sem, h_send, h_recv, h2_send, h2_recv, s_sem, r_send, r_recv,
    c_send, c_recv, e_send, e_recv, d_send, d_recv,
    f_send, f_recv, p_send, p_recv, g_send, g_recv, go,
):
    t, s = lax.axis_index("tm"), lax.axis_index("space")
    groups = T // GROUP
    LAST = T - 3
    MAIN = T - 2
    slot = lax.rem(t, GROUP)

    def home_of(group):
        return jnp.where(group == groups - 1, LAST, T - GROUP + 2 * group)

    home = home_of((t - slot) // GROUP)
    served = jnp.where(t == LAST, groups - 1, (t - (T - GROUP)) // 2)
    chain = (t == LAST) | ((t >= T - GROUP) & (lax.rem(t, 2) == 0) & (served < groups - 1))
    first = served * GROUP
    main = t == MAIN

    def beside(step):
        return lax.rem(s + step + S, S)

    barrier = pltpu.get_barrier_semaphore()

    def greet(tm, space):
        pl.semaphore_signal(barrier, inc=1, device_id=(tm, space), device_id_type=MESH)

    for step in (-1, 1):
        pl.when((s + step >= 0) & (s + step < S))(functools.partial(greet, t, s + step))
    pl.when(t < T - 1)(lambda: greet(t + 1, s))
    pl.when(t != home)(lambda: greet(home, s))
    pl.when((t >= GROUP) & (t != MAIN))(lambda: greet(MAIN, s))

    @pl.when(chain)
    def _():
        for step in (-2, 2):
            pl.when((s + step >= 0) & (s + step < S))(functools.partial(greet, t, s + step))

    @pl.when(main)
    def _():
        for z in range(S):
            for x in range(groups - 1):
                greet(T - GROUP + 2 * x, z)
            pl.when(s != z)(functools.partial(greet, t, z))

    fields = ((q_in, lv.at[0]), (u_in, st.at[0]), (w_in, st.at[1]), (v_in, st.at[2]),
              (cls_in, ints.at[0]), (msk_in, ints.at[1]))
    local = [pltpu.make_async_copy(src, dst.at[pl.ds(HF, W)], loc_sem.at[i])
             for i, (src, dst) in enumerate(fields)]
    for copy in local:
        copy.start()

    one = jnp.int32(1)
    zero = jnp.int32(0)

    def flag(condition):
        return jnp.where(condition, one, zero)

    expected = flag(s > 0) + flag(s < S - 1) + flag(t > 0)
    expected = expected + flag(chain) * (GROUP + flag(s > 1) + flag(s < S - 2))
    expected = expected + flag(chain & (t != LAST)) * S - flag(t == LAST) + flag(main) * (T - GROUP - 1 + S - 1)
    pl.semaphore_wait(barrier, expected)

    def halo(i, side):
        src, dst = fields[i]
        src_lo, dst_lo = ((0, HF + W), (W - HF, 0))[side]
        return pltpu.make_async_remote_copy(
            src_ref=src.at[pl.ds(src_lo, HF)], dst_ref=dst.at[pl.ds(dst_lo, HF)],
            send_sem=h_send.at[i, side], recv_sem=h_recv.at[i, side],
            device_id=(t, beside(2 * side - 1)), device_id_type=MESH)

    def halo2(side):
        src_lo, dst_lo = ((HF, HF + W), (W, 0))[side]
        return pltpu.make_async_remote_copy(
            src_ref=lv.at[4, pl.ds(src_lo, HF)], dst_ref=lv.at[4, pl.ds(dst_lo, HF)],
            send_sem=h2_send.at[side], recv_sem=h2_recv.at[side],
            device_id=(t, beside(2 * side - 1)), device_id_type=MESH)

    has_target = (s > 0, s < S - 1)
    order = (1, 2, 3, 4, 5, 0)
    for i in order:
        for side in (0, 1):
            pl.when(has_target[side])(lambda i=i, side=side: halo(i, side).start())

    for has, lo in ((s > 0, 0), (s < S - 1, HF + W)):
        @pl.when(jnp.logical_not(has))
        def _(lo=lo):
            edge = slice(lo, lo + HF)
            blank = jnp.zeros((HF, Z, Y), F32)
            for i in range(3):
                st[i, edge] = blank
            for i in range(2):
                ints[i, edge] = jnp.zeros((HF, Z, Y), jnp.int32)
            lv[0, edge] = blank
            lv[4, edge] = blank

    @pl.when(chain)
    def _():
        for n in range(GROUP):
            @pl.when(first + n != t)
            def _(n=n):
                pl.semaphore_signal(go, inc=1, device_id=(first + n, s), device_id_type=MESH)
        for has, lo in ((s > 1, 0), (s > 0, CW), (s < S - 1, 3 * CW), (s < S - 2, 4 * CW)):
            @pl.when(jnp.logical_not(has))
            def _(lo=lo):
                blank = jnp.zeros((CW, CZ, CY), F32)
                for i in range(5):
                    cs_win[i, lo : lo + CW] = blank

                for n in range(GROUP):
                    r_win[n, lo : lo + CW] = blank
                e_win[lo : lo + CW] = blank

    @pl.when(main)
    def _():
        margin = jnp.zeros((1, CZ, CY), F32)
        for lo in (0, S * CW + 1):
            for i in range(5):
                cs_full[i, lo : lo + 1] = margin
            for i in range(3):
                cur[i, lo : lo + 1] = margin
        for i in range(S):
            cur[0, 1 + i * CW : 1 + (i + 1) * CW] = jnp.zeros((CW, CZ, CY), F32)

    for copy in local:
        copy.wait()

    def widen(lo, n):
        own = slice(lo, lo + n)
        cls = ints[0, own]
        kappa = jnp.zeros(cls.shape, F32)
        for i in range(8):
            kappa = jnp.where(cls == i, kd[i], kappa)
        st[3, own] = kappa
        st[4, own] = ints[1, own].astype(F32)

    def sum_pairs(src, lo):
        for i in range(CW):
            pairs[i] = src[lo + 2 * i] + src[lo + 2 * i + 1]

    sum_pairs(lv.at[0], HF)
    s_own[...] = restrict(pairs[...])
    start_copy = pltpu.make_async_remote_copy(
        src_ref=s_own, dst_ref=s_next, send_sem=s_sem.at[0], recv_sem=s_sem.at[1],
        device_id=(lax.rem(t + T - 1, T), s), device_id_type=MESH)
    pl.when(t > 0)(lambda: start_copy.start())

    stat = [st.at[i] for i in range(5)]
    for lo, n in chunks(HF, HF + W, 2):
        widen(lo, n)
    for lo, n in chunks(HF + 1, HF + W - 1, 2):
        make_coefs(stat, coef, lo, n, 1.0)

    def to_slab(src, dst_of, send, recv, step):
        return pltpu.make_async_remote_copy(
            src_ref=src, dst_ref=dst_of((2 - step) * CW), send_sem=send, recv_sem=recv,
            device_id=(t, beside(step)), device_id_type=MESH)

    steps = (-2, 2, -1, 1)

    def there(step):
        return (s + step >= 0) & (s + step < S)

    def cs_copy(j):
        return to_slab(cs_own, lambda lo: cs_win.at[:, pl.ds(lo, CW)],
                       c_send.at[j], c_recv.at[j], steps[j])

    @pl.when(chain | main)
    def _():
        for i in range(5):
            sum_pairs(st.at[i], HF)
            cs_own[i] = restrict(pairs[...])

    @pl.when(chain)
    def _():
        for i in range(5):
            cs_win[i, 2 * CW : 3 * CW] = cs_own[i]
        for j in range(4):
            pl.when(there(steps[j]))(lambda j=j: cs_copy(j).start())

    def f_copy(z):
        return pltpu.make_async_remote_copy(
            src_ref=cs_own, dst_ref=cs_full.at[:, pl.ds(1 + s * CW, CW)],
            send_sem=f_send.at[z], recv_sem=f_recv.at[s],
            device_id=(MAIN, z), device_id_type=MESH)

    def f_arrival(z):
        return pltpu.make_async_remote_copy(
            src_ref=cs_own, dst_ref=cs_full.at[:, pl.ds(1 + z * CW, CW)],
            send_sem=f_send.at[z], recv_sem=f_recv.at[z],
            device_id=(MAIN, z), device_id_type=MESH)

    @pl.when(main)
    def _():
        cs_full[:, pl.ds(1 + s * CW, CW)] = cs_own[...]

    def fine(src, dst, shift, lo, hi):
        for i, n in chunks(lo, hi, 2):
            dst[i - shift : i - shift + n] = stencil(coef, src, i, n)

    def inner(base):
        for j in range(1, HF + 1):
            last = base + j == 2 * HF
            dst, shift = (ends, HF) if last else (lv.at[base + j], 0)
            fine(lv.at[base + j - 1], dst, shift, HF + j, HF + W - j)

    def outer(base):
        for j in range(1, HF + 1):
            last = base + j == 2 * HF
            dst, shift = (ends, HF) if last else (lv.at[base + j], 0)
            fine(lv.at[base + j - 1], dst, shift, j, HF + j)
            fine(lv.at[base + j - 1], dst, shift, HF + W - j, E - j)

    inner(0)
    for i in order:
        for side in (0, 1):
            pl.when(has_target[1 - side])(lambda i=i, side=side: halo(i, side).wait_recv())
    for lo in (0, HF + W):
        for i, n in chunks(lo, lo + HF, 2):
            widen(i, n)
    for lo in (1, HF + W - 1):
        for i, n in chunks(lo, lo + HF, 2):
            make_coefs(stat, coef, i, n, 1.0)
    outer(0)
    for side in (0, 1):
        pl.when(has_target[side])(lambda side=side: halo2(side).start())

    @pl.when(main)
    def _():
        for z in range(S):
            pl.when(s != z)(lambda z=z: f_copy(z).start())

    inner(HF)
    for side in (0, 1):
        pl.when(has_target[1 - side])(lambda side=side: halo2(side).wait_recv())
    outer(HF)

    sum_pairs(ends, 0)
    pl.when(t < T - 1)(lambda: start_copy.wait_recv())
    pl.when(t != home)(lambda: pl.semaphore_wait(go, 1))

    def r_copy(n, kind, j):
        step = (0,) + steps
        step = step[j]
        size = CW if step == 0 or (abs(step) == 1 and kind < 2) else CW // 2
        lo = CW - size if step > 0 else 0
        return pltpu.make_async_remote_copy(
            src_ref=r_own.at[pl.ds(lo, size)],
            dst_ref=r_win.at[n, pl.ds((2 - step) * CW + lo, size)],
            send_sem=r_send.at[j], recv_sem=r_recv.at[n, j],
            device_id=(home, beside(step)), device_id_type=MESH)

    pieces = ((0, 1, 2, 3, 4), (0, 3, 4), (0, 3, 4), (0,))

    def r_each(act):
        for kind in range(TURNS):
            @pl.when(lax.rem(slot, TURNS) == kind)
            def _(kind=kind):
                r_pieces(slot, kind, act, False)

    def r_pieces(n, kind, act, wait):
        for j in pieces[kind]:
            step = ((0,) + steps)[j]
            other = (first + n != t) if wait else (home != t)
            condition = other if step == 0 else there(-step if wait else step)
            pl.when(condition)(lambda j=j: act(r_copy(n, kind, j)))

    @pl.when(t < T - 1)
    def _():
        r_own[...] = restrict(pairs[...]) - s_next[...]

        @pl.when(t == home)
        def _():
            r_win[LAST % GROUP, 2 * CW : 3 * CW] = r_own[...]
        r_each(lambda copy: copy.start())

    def d_copy(n):
        return pltpu.make_async_remote_copy(
            src_ref=d_out.at[n], dst_ref=d_in, send_sem=d_send.at[n], recv_sem=d_recv,
            device_id=(first + n, s), device_id_type=MESH)

    def e_copy(j):
        return to_slab(e_win.at[pl.ds(2 * CW, CW)], lambda lo: e_win.at[pl.ds(lo, CW)],
                       e_send.at[j], e_recv.at[j], steps[j])

    def p_copy(z):
        return pltpu.make_async_remote_copy(
            src_ref=p_own, dst_ref=p_full.at[served, pl.ds(s * CW, CW)],
            send_sem=p_send.at[z], recv_sem=p_recv.at[served, s],
            device_id=(MAIN, z), device_id_type=MESH)

    def p_arrival(x, z):
        return pltpu.make_async_remote_copy(
            src_ref=p_own, dst_ref=p_full.at[x, pl.ds(z * CW, CW)],
            send_sem=p_send.at[z], recv_sem=p_recv.at[x, z],
            device_id=(MAIN, z), device_id_type=MESH)

    def turn(n, src, dst):
        kind = n % TURNS
        lo, hi = 4 * kind, WIN - 4 * kind
        for j in range(1, 4):
            for i, m in chunks(lo + j, hi - j, CW):
                wb[1 - j % 2, i : i + m] = stencil(ccoef, src, i, m)
            src = wb.at[1 - j % 2]
        own_lo, own_hi = 2 * CW, 3 * CW
        d_out[n] = stencil(ccoef, src, own_lo, CW)
        pl.when(first + n != t)(lambda: d_copy(n).start())

        @pl.when(first + n == t)
        def _():
            d_in[...] = d_out[n]

        if n == GROUP - 1:
            @pl.when(t != LAST)
            def _():
                r_pieces(n, kind, lambda copy: copy.wait_recv(), True)
                p_own[...] = d_out[n] + r_win[n, own_lo:own_hi]
                for z in range(S):
                    p_copy(z).start()
            return
        r_pieces(n, kind, lambda copy: copy.wait_recv(), True)
        into = slice(own_lo, own_hi)
        dst[into] = d_out[n] + r_win[n, into]
        for i, m in chunks(lo + 4, own_lo, CW) + chunks(own_hi, hi - 4, CW):
            dst[i : i + m] = stencil(ccoef, src, i, m) + r_win[n, i : i + m]

    @pl.when(chain)
    def _():
        for j in range(4):
            pl.when(there(-steps[j]))(lambda j=j: cs_copy(j).wait_recv())
        cstat = [cs_win.at[i] for i in range(5)]
        for lo, n in chunks(1, WIN - 1, 4):
            make_coefs(cstat, ccoef, lo, n, 0.5)

        r_pieces(0, 0, lambda copy: copy.wait_recv(), True)
        src = r_win.at[0]
        for n in range(1, TURNS):
            turn(n, src, wb.at[1] if n < TURNS - 1 else e_win)
            src = wb.at[1]
        for j in range(4):
            pl.when(there(steps[j]))(lambda j=j: e_copy(j).start())
        for j in range(4):
            pl.when(there(-steps[j]))(lambda j=j: e_copy(j).wait_recv())
        src = e_win
        for n in range(TURNS, GROUP):
            turn(n, src, wb.at[1])
            src = wb.at[1]

    def g_copy(m):
        return pltpu.make_async_remote_copy(
            src_ref=g_out.at[m], dst_ref=g_in, send_sem=g_send.at[m], recv_sem=g_recv,
            device_id=(m + GROUP, s), device_id_type=MESH)

    @pl.when(main)
    def _():
        for z in range(S):
            pl.when(s != z)(lambda z=z: f_arrival(z).wait_recv())
        fstat = [cs_full.at[i] for i in range(5)]
        for lo, n in chunks(1, S * CW + 1, 4):
            make_coefs(fstat, fcoef, lo, n, 0.5)

        def big_turn(m, carry):
            @pl.when(lax.rem(m, GROUP) == 0)
            def _():
                x = m // GROUP
                for z in range(S):
                    p_arrival(x, z).wait_recv()
                for i, n in chunks(0, S * CW, CW):
                    cur[0, i + 1 : i + 1 + n] = cur[0, i + 1 : i + 1 + n] + p_full[x, i : i + n]

            for a, b in ((0, 1), (1, 2), (2, 1), (1, 0)):
                for i, n in chunks(1, S * CW + 1, CW):
                    cur[b, i : i + n] = stencil(fcoef, cur.at[a], i, n)
            g_out[m] = cur[0, pl.ds(1 + s * CW, CW)]
            pl.when(m + GROUP != MAIN)(lambda: g_copy(m).start())
            return carry
        lax.fori_loop(0, T - GROUP, big_turn, 0)

    pl.when((slot > 0) & (t != LAST))(lambda: d_copy(slot).wait_recv())
    pl.when((t >= GROUP) & (t != MAIN))(lambda: g_copy(t - GROUP).wait_recv())

    @pl.when(main)
    def _():
        g_in[...] = g_out[MAIN - GROUP]

    @pl.when(slot == 0)
    def _():
        d_in[...] = jnp.zeros((CW, CZ, CY), F32)

    @pl.when(t >= GROUP)
    def _():
        d_in[...] = d_in[...] + g_in[...]

    fine_delta = prolong(d_in[...])
    for i in range(CW):
        out[2 * i] = ends[2 * i] + fine_delta[i]
        out[2 * i + 1] = ends[2 * i + 1] + fine_delta[i]

    for side in (0, 1):
        for i in order:
            pl.when(has_target[side])(lambda i=i, side=side: halo(i, side).wait_send())
        pl.when(has_target[side])(lambda side=side: halo2(side).wait_send())
    pl.when(t > 0)(lambda: start_copy.wait_send())
    pl.when(t < T - 1)(lambda: r_each(lambda copy: copy.wait_send()))

    @pl.when(chain)
    def _():
        for j in range(4):
            pl.when(there(steps[j]))(lambda j=j: cs_copy(j).wait_send())

            pl.when(there(steps[j]))(lambda j=j: e_copy(j).wait_send())
        for n in range(1, GROUP):
            pl.when(first + n != t)(lambda n=n: d_copy(n).wait_send())

        @pl.when(t != LAST)
        def _():
            for z in range(S):
                p_copy(z).wait_send()

    @pl.when(main)
    def _():
        for z in range(S):
            pl.when(s != z)(lambda z=z: f_copy(z).wait_send())

        def drain(m, carry):
            pl.when(m + GROUP != MAIN)(lambda: g_copy(m).wait_send())
            return carry
        lax.fori_loop(0, T - GROUP, drain, 0)


def shards(starts, u, w, v, cls, msk, kd):
    T, S = lax.axis_size("tm"), lax.axis_size("space")
    groups = T // GROUP
    dma = pltpu.SemaphoreType.DMA
    anywhere = pl.BlockSpec(memory_space=pl.ANY)
    slab = (CW, CZ, CY)
    result = pl.pallas_call(
        functools.partial(kernel, T, S),
        out_shape=jax.ShapeDtypeStruct((W, Z, Y), F32),
        in_specs=[anywhere] * 6 + [pl.BlockSpec(memory_space=pltpu.SMEM)],
        out_specs=pl.BlockSpec(memory_space=pltpu.VMEM),
        scratch_shapes=[
            pltpu.VMEM((5, E, Z, Y), F32),
            pltpu.VMEM((2, E, Z, Y), jnp.int32),
            pltpu.VMEM((8, E, Z, Y), F32),
            pltpu.VMEM((7, E, Z, Y), F32),
            pltpu.VMEM((W, Z, Y), F32),
            pltpu.VMEM((CW, Z, Y), F32),
            pltpu.VMEM(slab, F32),
            pltpu.VMEM(slab, F32),
            pltpu.VMEM(slab, F32),
            pltpu.VMEM((5,) + slab, F32),
            pltpu.VMEM((5, WIN, CZ, CY), F32),
            pltpu.VMEM((7, WIN, CZ, CY), F32),
            pltpu.VMEM((GROUP, WIN, CZ, CY), F32),
            pltpu.VMEM((WIN, CZ, CY), F32),
            pltpu.VMEM((2, WIN, CZ, CY), F32),
            pltpu.VMEM((GROUP,) + slab, F32),
            pltpu.VMEM(slab, F32),
            pltpu.VMEM((5, S * CW + 2, CZ, CY), F32),
            pltpu.VMEM((7, S * CW + 2, CZ, CY), F32),
            pltpu.VMEM(slab, F32),
            pltpu.VMEM((groups - 1, S * CW, CZ, CY), F32),
            pltpu.VMEM((3, S * CW + 2, CZ, CY), F32),
            pltpu.VMEM((T - GROUP,) + slab, F32),
            pltpu.VMEM(slab, F32),
            dma((6,)),
            dma((6, 2)), dma((6, 2)),
            dma((2,)), dma((2,)),
            dma((2,)),
            dma((5,)), dma((GROUP, 5)),
            dma((4,)), dma((4,)),
            dma((4,)), dma((4,)),
            dma((GROUP,)), dma(()),
            dma((S,)), dma((S,)),
            dma((S,)), dma((groups - 1, S)),
            dma((T - GROUP,)), dma(()),
            pltpu.SemaphoreType.REGULAR,
        ],
        compiler_params=pltpu.CompilerParams(
            collective_id=0, has_side_effects=True, vmem_limit_bytes=56 * 1024 * 1024),
    )(starts[0], u, w, v, cls, msk, kd)
    return result[None]


def solution(mesh):
    slabs = P("space", None, None)
    return jax.shard_map(
        shards, mesh=mesh,
        in_specs=(P("tm", "space", None, None),) + (slabs,) * 5 + (P(),),
        out_specs=P("tm", "space", None, None), check_vma=False)
```

```python
import functools

import jax
import jax.numpy as jnp
from jax import lax
from jax.experimental import pallas as pl
from jax.experimental.pallas import tpu as pltpu
from jax.sharding import PartitionSpec as P

MESH = pl.DeviceIdType.MESH
W, HF, Z, Y = 16, 4, 16, 256
E = W + 2 * HF
CW, CZ, CY = W // 2, Z // 2, Y // 2
WIN = 5 * CW
TURNS = 4
GROUP = 2 * TURNS
HALF = TURNS
F32 = jnp.float32


def up(x, axis):
    return pltpu.roll(x, x.shape[axis] - 1, axis)


def down(x, axis):
    return pltpu.roll(x, 1, axis)


def face(speed_a, speed_b, mix_a, mix_b, open_face, scale):
    f = 0.5 * (speed_a + speed_b) * open_face
    h = (0.5 * scale) * (mix_a + mix_b) * open_face
    return jnp.maximum(f, 0.0) + h, h - jnp.minimum(f, 0.0)


def make_coefs(stat, coef, lo, n, scale):
    u, w, v, k, m = stat
    ka, kb = k[lo - 1 : lo + n], k[lo : lo + n + 1]
    ma, mb = m[lo - 1 : lo + n], m[lo : lo + n + 1]
    a, b = face(u[lo - 1 : lo + n], u[lo : lo + n + 1], ka, kb, ma * mb, scale)
    own = slice(lo, lo + n)
    coef[1, own] = a[:n]
    coef[2, own] = b[1:]
    centre = 1.0 - (a[1:] + b[:n])
    kc, mc = kb[:n], mb[:n]
    for axis, field, low, high in ((1, w, 3, 4), (2, v, 5, 6)):
        c = field[own]
        extent = c.shape[axis]
        inside = lax.broadcasted_iota(jnp.int32, c.shape, axis) < extent - 1
        open_face = jnp.where(inside, mc * up(mc, axis), 0.0)
        a, b = face(c, up(c, axis), kc, up(kc, axis), open_face, scale)
        coef[low, own] = down(a, axis)
        coef[high, own] = b
        centre = centre - (a + down(b, axis))
    coef[0, own] = centre


def stencil(coef, q, lo, n):
    own = slice(lo, lo + n)
    c = q[own]
    x = coef[1, own] * q[lo - 1 : lo + n - 1] + coef[2, own] * q[lo + 1 : lo + n + 1]
    z = coef[3, own] * down(c, 1) + coef[4, own] * up(c, 1)
    y = coef[5, own] * down(c, 2) + coef[6, own] * up(c, 2)
    return (coef[0, own] * c + x) + (z + y)


def chunks(lo, hi, size):
    return [(i, min(size, hi - i)) for i in range(lo, hi, size)]


def pick(rows, cols, along):
    r = lax.broadcasted_iota(jnp.int32, (rows, cols), 0)
    c = lax.broadcasted_iota(jnp.int32, (rows, cols), 1)
    return jnp.where((r >> 1) == c if along == 0 else (c >> 1) == r, 1.0, 0.0).astype(F32)


def mul(a, b):
    return jnp.dot(a, b, precision=lax.Precision.HIGHEST, preferred_element_type=F32)


def restrict(pairs):
    flat = pairs.reshape(CW * Z, Y)
    narrow = mul(flat, pick(Y, CY, 0))
    short = mul(pick(CW * CZ, CW * Z, 1), narrow)
    return (0.125 * short).reshape(CW, CZ, CY)


def prolong(coarse):
    flat = mul(coarse.reshape(CW * CZ, CY), pick(CY, Y, 1))
    return mul(pick(CW * Z, CW * CZ, 0), flat).reshape(CW, Z, Y)


def kernel(
    T, S,
    q_in, u_in, w_in, v_in, cls_in, msk_in, kd,
    out,
    st, ints, lv, coef, ends, pairs, s_own, s_next, r_own,
    cs_own, cs_win, ccoef, r_win, e_win, wb, d_out, d_in,
    cs_full, fcoef, p_own, p_full, cur, g_out, g_in,
    loc_sem, h_send, h_recv, m_send, m_recv, h2_send, h2_recv, s_sem, r_send, r_recv,
    c_send, c_recv, e_send, e_recv, d_send, d_recv,
    f_send, f_recv, p_send, p_recv, g_send, g_recv, go,
):
    t, s = lax.axis_index("tm"), lax.axis_index("space")
    groups = T // GROUP + 1
    LAST = T - 9
    MAIN = T - 2
    homes = [T - 8, T - 6, T - 4, T - 11][: groups - 1] + [LAST]
    slot = jnp.where(t < HALF, t + HALF, lax.rem(t, GROUP))
    group = jnp.where(t < HALF, 0, t // GROUP + 1)

    def among(pairs, other):
        value = jnp.int32(other)
        for condition, choice in pairs:
            value = jnp.where(condition, jnp.int32(choice), value)
        return value

    home = among([(group == g, row) for g, row in enumerate(homes)], 0)
    served = among([(t == row, g) for g, row in enumerate(homes)], -1)
    chain = served >= 0
    final = served == groups - 1
    first = jnp.where(served == 0, -HALF, (served - 1) * GROUP)
    short = served < 2
    main = t == MAIN
    helper = t == T - 10
    core = lax.rem(t, 2)
    mate = t + 1 - 2 * core

    def member(n):
        return jnp.logical_not(short) if n < HALF else served >= 0

    def beside(step):
        return lax.rem(s + step + S, S)

    barrier = pltpu.get_barrier_semaphore()

    def greet(tm, space):
        pl.semaphore_signal(barrier, inc=1, device_id=(tm, space), device_id_type=MESH)

    for step in (-1, 1):
        pl.when((s + step >= 0) & (s + step < S))(functools.partial(greet, t, s + step))
    pl.when(t < T - 1)(lambda: greet(t + 1, s))
    greet(mate, s)
    pl.when(t != home)(lambda: greet(home, s))
    pl.when((t >= HALF) & (t != MAIN))(lambda: greet(MAIN, s))

    @pl.when(chain)
    def _():
        for step in (-2, 2):
            pl.when((s + step >= 0) & (s + step < S))(functools.partial(greet, t, s + step))

    @pl.when(main)
    def _():
        for z in range(S):
            for row in homes[:-1] + [T - 10]:
                greet(row, z)
            pl.when(s != z)(functools.partial(greet, t, z))

    fields = ((q_in, lv.at[0]), (u_in, st.at[0]), (w_in, st.at[1]), (v_in, st.at[2]),
              (cls_in, ints.at[0]), (msk_in, ints.at[1]))
    local = [pltpu.make_async_copy(src, dst.at[pl.ds(HF, W)], loc_sem.at[i])
             for i, (src, dst) in enumerate(fields)]
    for copy in local:
        copy.start()

    one = jnp.int32(1)
    zero = jnp.int32(0)

    def flag(condition):
        return jnp.where(condition, one, zero)

    expected = 1 + flag(s > 0) + flag(s < S - 1) + flag(t > 0)
    expected = expected + flag(chain) * (flag(s > 1) + flag(s < S - 2))
    expected = expected + flag(chain) * (GROUP - HALF * flag(short)) - flag(chain & (home == t))
    expected = expected + flag(chain & (t != LAST)) * S + flag(helper) * S + flag(main) * (T - HALF - 1 + S - 1)
    pl.semaphore_wait(barrier, expected)

    PART = HF // 2

    def halo(i, side):
        src, dst = fields[i]
        src_lo, dst_lo = ((0, HF + W), (W - HF, 0))[side]
        n, skip = (HF, 0) if i == 0 else (PART, core * PART)
        return pltpu.make_async_remote_copy(
            src_ref=src.at[pl.ds(src_lo + skip, n)], dst_ref=dst.at[pl.ds(dst_lo + skip, n)],
            send_sem=h_send.at[i, side], recv_sem=h_recv.at[i, side],
            device_id=(t, beside(2 * side - 1)), device_id_type=MESH)

    def share(i, side, which):
        dst = fields[i][1]
        part = dst.at[pl.ds((HF + W, 0)[side] + which * PART, PART)]
        return pltpu.make_async_remote_copy(
            src_ref=part, dst_ref=part, send_sem=m_send.at[i, side], recv_sem=m_recv.at[i, side],
            device_id=(mate, s), device_id_type=MESH)

    def halo2(side):
        src_lo, dst_lo = ((HF, HF + W), (W, 0))[side]
        return pltpu.make_async_remote_copy(
            src_ref=lv.at[4, pl.ds(src_lo, HF)], dst_ref=lv.at[4, pl.ds(dst_lo, HF)],
            send_sem=h2_send.at[side], recv_sem=h2_recv.at[side],
            device_id=(t, beside(2 * side - 1)), device_id_type=MESH)

    has_target = (s > 0, s < S - 1)
    order = (1, 2, 3, 4, 5, 0)
    for i in order:
        for side in (0, 1):
            pl.when(has_target[side])(lambda i=i, side=side: halo(i, side).start())

    for has, lo in ((s > 0, 0), (s < S - 1, HF + W)):
        @pl.when(jnp.logical_not(has))
        def _(lo=lo):
            edge = slice(lo, lo + HF)
            blank = jnp.zeros((HF, Z, Y), F32)
            for i in range(3):
                st[i, edge] = blank
            for i in range(2):
                ints[i, edge] = jnp.zeros((HF, Z, Y), jnp.int32)
            lv[0, edge] = blank
            lv[4, edge] = blank

    @pl.when(chain)
    def _():
        for n in range(GROUP):
            @pl.when(member(n) & (first + n != t))
            def _(n=n):
                pl.semaphore_signal(go, inc=1, device_id=(first + n, s), device_id_type=MESH)
        for has, lo in ((s > 1, 0), (s > 0, CW), (s < S - 1, 3 * CW), (s < S - 2, 4 * CW)):
            @pl.when(jnp.logical_not(has))
            def _(lo=lo):
                blank = jnp.zeros((CW, CZ, CY), F32)
                for i in range(5):
                    cs_win[i, lo : lo + CW] = blank

                for n in range(GROUP):
                    r_win[n, lo : lo + CW] = blank
                e_win[lo : lo + CW] = blank

    @pl.when(main)
    def _():
        margin = jnp.zeros((1, CZ, CY), F32)
        for lo in (0, S * CW + 1):
            for i in range(5):
                cs_full[i, lo : lo + 1] = margin
            for i in range(3):
                cur[i, lo : lo + 1] = margin
        for i in range(S):
            cur[0, 1 + i * CW : 1 + (i + 1) * CW] = jnp.zeros((CW, CZ, CY), F32)

    for copy in local:
        copy.wait()

    def widen(lo, n):
        own = slice(lo, lo + n)
        cls = ints[0, own]
        kappa = jnp.zeros(cls.shape, F32)
        for i in range(8):
            kappa = jnp.where(cls == i, kd[i], kappa)
        st[3, own] = kappa
        st[4, own] = ints[1, own].astype(F32)

    def sum_pairs(src, lo):
        for i in range(CW):
            pairs[i] = src[lo + 2 * i] + src[lo + 2 * i + 1]

    sum_pairs(lv.at[0], HF)
    s_own[...] = restrict(pairs[...])
    start_copy = pltpu.make_async_remote_copy(
        src_ref=s_own, dst_ref=s_next, send_sem=s_sem.at[0], recv_sem=s_sem.at[1],
        device_id=(lax.rem(t + T - 1, T), s), device_id_type=MESH)
    pl.when(t > 0)(lambda: start_copy.start())

    stat = [st.at[i] for i in range(5)]
    for lo, n in chunks(HF, HF + W, 2):
        widen(lo, n)
    for lo, n in chunks(HF + 1, HF + W - 1, 2):
        make_coefs(stat, coef, lo, n, 1.0)

    def to_slab(src, dst_of, send, recv, step):
        return pltpu.make_async_remote_copy(
            src_ref=src, dst_ref=dst_of((2 - step) * CW), send_sem=send, recv_sem=recv,
            device_id=(t, beside(step)), device_id_type=MESH)

    steps = (-2, 2, -1, 1)

    def there(step):
        return (s + step >= 0) & (s + step < S)

    def cs_copy(j):
        return to_slab(cs_own, lambda lo: cs_win.at[:, pl.ds(lo, CW)],
                       c_send.at[j], c_recv.at[j], steps[j])

    @pl.when(chain | main | helper)
    def _():
        for i in range(5):
            sum_pairs(st.at[i], HF)
            cs_own[i] = restrict(pairs[...])

    @pl.when(chain)
    def _():
        for i in range(5):
            cs_win[i, 2 * CW : 3 * CW] = cs_own[i]
        for j in range(4):
            pl.when(there(steps[j]))(lambda j=j: cs_copy(j).start())

    def f_copy(z):
        return pltpu.make_async_remote_copy(
            src_ref=cs_own, dst_ref=cs_full.at[:, pl.ds(1 + s * CW, CW)],
            send_sem=f_send.at[z], recv_sem=f_recv.at[s],
            device_id=(MAIN, z), device_id_type=MESH)

    def f_arrival(z):
        return pltpu.make_async_remote_copy(
            src_ref=cs_own, dst_ref=cs_full.at[:, pl.ds(1 + z * CW, CW)],
            send_sem=f_send.at[z], recv_sem=f_recv.at[z],
            device_id=(MAIN, z), device_id_type=MESH)

    def f_each(who, act):
        for z in range(S):
            gap = lax.rem(z - s + S, S)
            near = (gap <= 2) | (gap >= S - 2)
            wanted = jnp.logical_not(near) if who is helper else near & (gap != 0)
            pl.when(who & wanted)(lambda z=z: act(z))

    f_each(helper, lambda z: f_copy(z).start())

    @pl.when(main)
    def _():
        cs_full[:, pl.ds(1 + s * CW, CW)] = cs_own[...]

    def fine(src, dst, shift, lo, hi):
        for i, n in chunks(lo, hi, 2):
            dst[i - shift : i - shift + n] = stencil(coef, src, i, n)

    def inner(base):
        for j in range(1, HF + 1):
            last = base + j == 2 * HF
            dst, shift = (ends, HF) if last else (lv.at[base + j], 0)
            fine(lv.at[base + j - 1], dst, shift, HF + j, HF + W - j)

    def outer(base):
        for j in range(1, HF + 1):
            last = base + j == 2 * HF
            dst, shift = (ends, HF) if last else (lv.at[base + j], 0)
            fine(lv.at[base + j - 1], dst, shift, j, HF + j)
            fine(lv.at[base + j - 1], dst, shift, HF + W - j, E - j)

    inner(0)
    for i in order:
        for side in (0, 1):
            @pl.when(has_target[1 - side])
            def _(i=i, side=side):
                halo(i, side).wait_recv()
                if i > 0:
                    share(i, side, core).start()
    for i in order[:-1]:
        for side in (0, 1):
            pl.when(has_target[1 - side])(
                lambda i=i, side=side: share(i, side, 1 - core).wait_recv())
    for lo in (0, HF + W):
        for i, n in chunks(lo, lo + HF, 2):
            widen(i, n)
    for lo in (1, HF + W - 1):
        for i, n in chunks(lo, lo + HF, 2):
            make_coefs(stat, coef, i, n, 1.0)
    outer(0)
    for side in (0, 1):
        pl.when(has_target[side])(lambda side=side: halo2(side).start())

    f_each(main, lambda z: f_copy(z).start())
    inner(HF)
    for side in (0, 1):
        pl.when(has_target[1 - side])(lambda side=side: halo2(side).wait_recv())
    outer(HF)

    sum_pairs(ends, 0)
    pl.when(t < T - 1)(lambda: start_copy.wait_recv())
    pl.when(t != home)(lambda: pl.semaphore_wait(go, 1))

    def r_copy(n, kind, j):
        step = (0,) + steps
        step = step[j]
        size = CW if step == 0 or (abs(step) == 1 and kind < 2) else CW // 2
        lo = CW - size if step > 0 else 0
        return pltpu.make_async_remote_copy(
            src_ref=r_own.at[pl.ds(lo, size)],
            dst_ref=r_win.at[n, pl.ds((2 - step) * CW + lo, size)],
            send_sem=r_send.at[j], recv_sem=r_recv.at[n, j],
            device_id=(home, beside(step)), device_id_type=MESH)

    pieces = ((0, 1, 2, 3, 4), (0, 3, 4), (0, 3, 4), (0,))

    def r_each(act):
        for kind in range(TURNS):
            @pl.when(lax.rem(slot, TURNS) == kind)
            def _(kind=kind):
                r_pieces(slot, kind, act, False)

    def r_pieces(n, kind, act, wait):
        for j in pieces[kind]:
            step = ((0,) + steps)[j]
            other = (first + n != t) if wait else (home != t)
            condition = other if step == 0 else there(-step if wait else step)
            pl.when(condition)(lambda j=j: act(r_copy(n, kind, j)))

    @pl.when(t < T - 1)
    def _():
        r_own[...] = restrict(pairs[...]) - s_next[...]

        @pl.when(t == home)
        def _():
            r_win[slot, 2 * CW : 3 * CW] = r_own[...]
        r_each(lambda copy: copy.start())

    def d_copy(n):
        return pltpu.make_async_remote_copy(
            src_ref=d_out.at[n], dst_ref=d_in, send_sem=d_send.at[n], recv_sem=d_recv,
            device_id=(first + n, s), device_id_type=MESH)

    def e_copy(j):
        return to_slab(e_win.at[pl.ds(2 * CW, CW)], lambda lo: e_win.at[pl.ds(lo, CW)],
                       e_send.at[j], e_recv.at[j], steps[j])

    def p_copy(z):
        return pltpu.make_async_remote_copy(
            src_ref=p_own, dst_ref=p_full.at[served, pl.ds(s * CW, CW)],
            send_sem=p_send.at[z], recv_sem=p_recv.at[served, s],
            device_id=(MAIN, z), device_id_type=MESH)

    def p_arrival(x, z):
        return pltpu.make_async_remote_copy(
            src_ref=p_own, dst_ref=p_full.at[x, pl.ds(z * CW, CW)],
            send_sem=p_send.at[z], recv_sem=p_recv.at[x, z],
            device_id=(MAIN, z), device_id_type=MESH)

    def turn(n, src, dst):
        kind = n % TURNS
        lo, hi = 4 * kind, WIN - 4 * kind
        for j in range(1, 4):
            for i, m in chunks(lo + j, hi - j, CW):
                wb[1 - j % 2, i : i + m] = stencil(ccoef, src, i, m)
            src = wb.at[1 - j % 2]
        own_lo, own_hi = 2 * CW, 3 * CW
        d_out[n] = stencil(ccoef, src, own_lo, CW)
        pl.when(first + n != t)(lambda: d_copy(n).start())

        @pl.when(first + n == t)
        def _():
            d_in[...] = d_out[n]

        def arrivals():
            r_pieces(n, kind, lambda copy: copy.wait_recv(), True)

        if n == GROUP - 1:
            @pl.when(jnp.logical_not(final))
            def _():
                arrivals()
                p_own[...] = d_out[n] + r_win[n, own_lo:own_hi]
                for z in range(S):
                    p_copy(z).start()
            return
        into = slice(own_lo, own_hi)
        arrivals()
        dst[into] = d_out[n] + r_win[n, into]
        for i, m in chunks(lo + 4, own_lo, CW) + chunks(own_hi, hi - 4, CW):
            dst[i : i + m] = stencil(ccoef, src, i, m) + r_win[n, i : i + m]

    @pl.when(chain)
    def _():
        for j in range(4):
            pl.when(there(-steps[j]))(lambda j=j: cs_copy(j).wait_recv())
        cstat = [cs_win.at[i] for i in range(5)]
        for lo, n in chunks(1, WIN - 1, 4):
            make_coefs(cstat, ccoef, lo, n, 0.5)

        @pl.when(jnp.logical_not(short))
        def _():
            r_pieces(0, 0, lambda copy: copy.wait_recv(), True)
            src = r_win.at[0]
            for n in range(1, HALF):
                turn(n, src, wb.at[1] if n < HALF - 1 else e_win)
                src = wb.at[1]
            for j in range(4):
                pl.when(there(steps[j]))(lambda j=j: e_copy(j).start())
            for j in range(4):
                pl.when(there(-steps[j]))(lambda j=j: e_copy(j).wait_recv())
            turn(HALF, e_win, wb.at[1])

        @pl.when(short)
        def _():
            r_pieces(HALF, 0, lambda copy: copy.wait_recv(), True)
            for i, m in chunks(4, WIN - 4, CW):
                wb[1, i : i + m] = r_win[HALF, i : i + m]

        for n in range(HALF + 1, GROUP):
            turn(n, wb.at[1], wb.at[1])

    def g_copy(m):
        return pltpu.make_async_remote_copy(
            src_ref=g_out.at[m], dst_ref=g_in, send_sem=g_send.at[m], recv_sem=g_recv,
            device_id=(m + HALF, s), device_id_type=MESH)

    @pl.when(main)
    def _():
        for z in range(S):
            pl.when(s != z)(lambda z=z: f_arrival(z).wait_recv())
        fstat = [cs_full.at[i] for i in range(5)]
        for lo, n in chunks(1, S * CW + 1, 4):
            make_coefs(fstat, fcoef, lo, n, 0.5)

        def big_turn(m, carry):
            @pl.when((m == 0) | (lax.rem(m, GROUP) == HALF))
            def _():
                x = (m + HALF) // GROUP
                for z in range(S):
                    p_arrival(x, z).wait_recv()
                for i, n in chunks(0, S * CW, CW):
                    cur[0, i + 1 : i + 1 + n] = cur[0, i + 1 : i + 1 + n] + p_full[x, i : i + n]

            for a, b in ((0, 1), (1, 2), (2, 1), (1, 0)):
                for i, n in chunks(1, S * CW + 1, CW):
                    cur[b, i : i + n] = stencil(fcoef, cur.at[a], i, n)
            g_out[m] = cur[0, pl.ds(1 + s * CW, CW)]
            pl.when(m + HALF != MAIN)(lambda: g_copy(m).start())
            return carry
        lax.fori_loop(0, T - HALF, big_turn, 0)

    start = (t == 0) | (t == HALF) | (slot == 0)
    pl.when(jnp.logical_not(start) & (t != home))(lambda: d_copy(slot).wait_recv())
    pl.when((t >= HALF) & (t != MAIN))(lambda: g_copy(t - HALF).wait_recv())

    @pl.when(main)
    def _():
        g_in[...] = g_out[MAIN - HALF]

    @pl.when(start)
    def _():
        d_in[...] = jnp.zeros((CW, CZ, CY), F32)

    @pl.when(t >= HALF)
    def _():
        d_in[...] = d_in[...] + g_in[...]

    fine_delta = prolong(d_in[...])
    for i in range(CW):
        out[2 * i] = ends[2 * i] + fine_delta[i]
        out[2 * i + 1] = ends[2 * i + 1] + fine_delta[i]

    for side in (0, 1):
        for i in order:
            pl.when(has_target[side])(lambda i=i, side=side: halo(i, side).wait_send())
            if i > 0:
                pl.when(has_target[1 - side])(
                    lambda i=i, side=side: share(i, side, core).wait_send())
        pl.when(has_target[side])(lambda side=side: halo2(side).wait_send())
    pl.when(t > 0)(lambda: start_copy.wait_send())
    pl.when(t < T - 1)(lambda: r_each(lambda copy: copy.wait_send()))

    @pl.when(chain)
    def _():
        for j in range(4):
            pl.when(there(steps[j]))(lambda j=j: cs_copy(j).wait_send())

            pl.when(there(steps[j]) & jnp.logical_not(short))(
                lambda j=j: e_copy(j).wait_send())
        for n in range(1, GROUP):
            begun = jnp.logical_not(short) if n <= HALF else chain
            pl.when(begun & (first + n != t))(lambda n=n: d_copy(n).wait_send())

        @pl.when(t != LAST)
        def _():
            for z in range(S):
                p_copy(z).wait_send()

    f_each(helper, lambda z: f_copy(z).wait_send())
    f_each(main, lambda z: f_copy(z).wait_send())

    @pl.when(main)
    def _():
        def drain(m, carry):
            pl.when(m + HALF != MAIN)(lambda: g_copy(m).wait_send())
            return carry
        lax.fori_loop(0, T - HALF, drain, 0)


def shards(starts, u, w, v, cls, msk, kd):
    T, S = lax.axis_size("tm"), lax.axis_size("space")
    groups = T // GROUP + 1
    dma = pltpu.SemaphoreType.DMA
    anywhere = pl.BlockSpec(memory_space=pl.ANY)
    slab = (CW, CZ, CY)
    result = pl.pallas_call(
        functools.partial(kernel, T, S),
        out_shape=jax.ShapeDtypeStruct((W, Z, Y), F32),
        in_specs=[anywhere] * 6 + [pl.BlockSpec(memory_space=pltpu.SMEM)],
        out_specs=pl.BlockSpec(memory_space=pltpu.VMEM),
        scratch_shapes=[
            pltpu.VMEM((5, E, Z, Y), F32),
            pltpu.VMEM((2, E, Z, Y), jnp.int32),
            pltpu.VMEM((8, E, Z, Y), F32),
            pltpu.VMEM((7, E, Z, Y), F32),
            pltpu.VMEM((W, Z, Y), F32),
            pltpu.VMEM((CW, Z, Y), F32),
            pltpu.VMEM(slab, F32),
            pltpu.VMEM(slab, F32),
            pltpu.VMEM(slab, F32),
            pltpu.VMEM((5,) + slab, F32),
            pltpu.VMEM((5, WIN, CZ, CY), F32),
            pltpu.VMEM((7, WIN, CZ, CY), F32),
            pltpu.VMEM((GROUP, WIN, CZ, CY), F32),
            pltpu.VMEM((WIN, CZ, CY), F32),
            pltpu.VMEM((2, WIN, CZ, CY), F32),
            pltpu.VMEM((GROUP,) + slab, F32),
            pltpu.VMEM(slab, F32),
            pltpu.VMEM((5, S * CW + 2, CZ, CY), F32),
            pltpu.VMEM((7, S * CW + 2, CZ, CY), F32),
            pltpu.VMEM(slab, F32),
            pltpu.VMEM((groups - 1, S * CW, CZ, CY), F32),
            pltpu.VMEM((3, S * CW + 2, CZ, CY), F32),
            pltpu.VMEM((T - HALF,) + slab, F32),
            pltpu.VMEM(slab, F32),
            dma((6,)),
            dma((6, 2)), dma((6, 2)),
            dma((6, 2)), dma((6, 2)),
            dma((2,)), dma((2,)),
            dma((2,)),
            dma((5,)), dma((GROUP, 5)),
            dma((4,)), dma((4,)),
            dma((4,)), dma((4,)),
            dma((GROUP,)), dma(()),
            dma((S,)), dma((S,)),
            dma((S,)), dma((groups - 1, S)),
            dma((T - HALF,)), dma(()),
            pltpu.SemaphoreType.REGULAR,
        ],
        compiler_params=pltpu.CompilerParams(
            collective_id=0, has_side_effects=True, vmem_limit_bytes=56 * 1024 * 1024),
    )(starts[0], u, w, v, cls, msk, kd)
    return result[None]


def solution(mesh):
    slabs = P("space", None, None)
    return jax.shard_map(
        shards, mesh=mesh,
        in_specs=(P("tm", "space", None, None),) + (slabs,) * 5 + (P(),),
        out_specs=P("tm", "space", None, None), check_vma=False)
```

```python
import functools

import jax
import jax.numpy as jnp
from jax import lax
from jax.experimental import pallas as pl
from jax.experimental.pallas import tpu as pltpu
from jax.sharding import PartitionSpec as P

MESH = pl.DeviceIdType.MESH
W, HF, Z, Y = 16, 4, 16, 256
E = W + 2 * HF
CW, CZ, CY = W // 2, Z // 2, Y // 2
WIN = 5 * CW
TURNS = 4
GROUP = 2 * TURNS
HALF = TURNS
F32 = jnp.float32


def up(x, axis):
    return pltpu.roll(x, x.shape[axis] - 1, axis)


def down(x, axis):
    return pltpu.roll(x, 1, axis)


def face(speed_a, speed_b, mix_a, mix_b, open_face, scale):
    f = 0.5 * (speed_a + speed_b) * open_face
    h = (0.5 * scale) * (mix_a + mix_b) * open_face
    return jnp.maximum(f, 0.0) + h, h - jnp.minimum(f, 0.0)


def make_coefs(stat, coef, lo, n, scale):
    u, w, v, k, m = stat
    ka, kb = k[lo - 1 : lo + n], k[lo : lo + n + 1]
    ma, mb = m[lo - 1 : lo + n], m[lo : lo + n + 1]
    a, b = face(u[lo - 1 : lo + n], u[lo : lo + n + 1], ka, kb, ma * mb, scale)
    own = slice(lo, lo + n)
    coef[1, own] = a[:n]
    coef[2, own] = b[1:]
    centre = 1.0 - (a[1:] + b[:n])
    kc, mc = kb[:n], mb[:n]
    for axis, field, low, high in ((1, w, 3, 4), (2, v, 5, 6)):
        c = field[own]
        extent = c.shape[axis]
        inside = lax.broadcasted_iota(jnp.int32, c.shape, axis) < extent - 1
        open_face = jnp.where(inside, mc * up(mc, axis), 0.0)
        a, b = face(c, up(c, axis), kc, up(kc, axis), open_face, scale)
        coef[low, own] = down(a, axis)
        coef[high, own] = b
        centre = centre - (a + down(b, axis))
    coef[0, own] = centre


def stencil(coef, q, lo, n):
    own = slice(lo, lo + n)
    c = q[own]
    x = coef[1, own] * q[lo - 1 : lo + n - 1] + coef[2, own] * q[lo + 1 : lo + n + 1]
    z = coef[3, own] * down(c, 1) + coef[4, own] * up(c, 1)
    y = coef[5, own] * down(c, 2) + coef[6, own] * up(c, 2)
    return (coef[0, own] * c + x) + (z + y)


def chunks(lo, hi, size):
    return [(i, min(size, hi - i)) for i in range(lo, hi, size)]


def pick(rows, cols, along):
    r = lax.broadcasted_iota(jnp.int32, (rows, cols), 0)
    c = lax.broadcasted_iota(jnp.int32, (rows, cols), 1)
    return jnp.where((r >> 1) == c if along == 0 else (c >> 1) == r, 1.0, 0.0).astype(F32)


def mul(a, b):
    return jnp.dot(a, b, precision=lax.Precision.HIGHEST, preferred_element_type=F32)


def restrict(pairs):
    flat = pairs.reshape(CW * Z, Y)
    narrow = mul(flat, pick(Y, CY, 0))
    short = mul(pick(CW * CZ, CW * Z, 1), narrow)
    return (0.125 * short).reshape(CW, CZ, CY)


def prolong(coarse):
    flat = mul(coarse.reshape(CW * CZ, CY), pick(CY, Y, 1))
    return mul(pick(CW * Z, CW * CZ, 0), flat).reshape(CW, Z, Y)


def kernel(
    T, S,
    q_in, u_in, w_in, v_in, cls_in, msk_in, kd,
    ends_out, delta_out,
    st, ints, lv, coef, ends, pairs, s_own, s_next, r_own,
    cs_own, cs_win, ccoef, r_win, e_win, wb, d_out, d_in,
    cs_full, fcoef, p_own, p_full, cur, g_out, g_in,
    loc_sem, h_send, h_recv, m_send, m_recv, h2_send, h2_recv, s_sem, r_send, r_recv,
    c_send, c_recv, e_send, e_recv, d_send, d_recv,
    f_send, f_recv, p_send, p_recv, g_send, g_recv, go,
):
    t, s = lax.axis_index("tm"), lax.axis_index("space")
    groups = T // GROUP + 1
    LAST = T - 9
    MAIN = T - 2
    homes = [T - 8, T - 6, T - 4, T - 11][: groups - 1] + [LAST]
    slot = jnp.where(t < HALF, t + HALF, lax.rem(t, GROUP))
    group = jnp.where(t < HALF, 0, t // GROUP + 1)

    def among(pairs, other):
        value = jnp.int32(other)
        for condition, choice in pairs:
            value = jnp.where(condition, jnp.int32(choice), value)
        return value

    home = among([(group == g, row) for g, row in enumerate(homes)], 0)
    served = among([(t == row, g) for g, row in enumerate(homes)], -1)
    chain = served >= 0
    final = served == groups - 1
    first = jnp.where(served == 0, -HALF, (served - 1) * GROUP)
    short = served < 2
    main = t == MAIN
    helper = t == T - 10
    core = lax.rem(t, 2)
    mate = t + 1 - 2 * core

    def member(n):
        return jnp.logical_not(short) if n < HALF else served >= 0

    def beside(step):
        return lax.rem(s + step + S, S)

    barrier = pltpu.get_barrier_semaphore()

    def greet(tm, space):
        pl.semaphore_signal(barrier, inc=1, device_id=(tm, space), device_id_type=MESH)

    for step in (-1, 1):
        pl.when((s + step >= 0) & (s + step < S))(functools.partial(greet, t, s + step))
    pl.when(t < T - 1)(lambda: greet(t + 1, s))
    greet(mate, s)
    pl.when(t != home)(lambda: greet(home, s))
    pl.when((t >= HALF) & (t != MAIN))(lambda: greet(MAIN, s))

    @pl.when(chain)
    def _():
        for step in (-2, 2):
            pl.when((s + step >= 0) & (s + step < S))(functools.partial(greet, t, s + step))

    @pl.when(main)
    def _():
        for z in range(S):
            for row in homes[:-1] + [T - 10]:
                greet(row, z)
            pl.when(s != z)(functools.partial(greet, t, z))

    fields = ((q_in, lv.at[0]), (u_in, st.at[0]), (w_in, st.at[1]), (v_in, st.at[2]),
              (cls_in, ints.at[0]), (msk_in, ints.at[1]))
    local = [pltpu.make_async_copy(src, dst.at[pl.ds(HF, W)], loc_sem.at[i])
             for i, (src, dst) in enumerate(fields)]
    for copy in local:
        copy.start()

    one = jnp.int32(1)
    zero = jnp.int32(0)

    def flag(condition):
        return jnp.where(condition, one, zero)

    expected = 1 + flag(s > 0) + flag(s < S - 1) + flag(t > 0)
    expected = expected + flag(chain) * (flag(s > 1) + flag(s < S - 2))
    expected = expected + flag(chain) * (GROUP - HALF * flag(short)) - flag(chain & (home == t))
    expected = expected + flag(chain & (t != LAST)) * S + flag(helper) * S + flag(main) * (T - HALF - 1 + S - 1)
    pl.semaphore_wait(barrier, expected)

    PART = HF // 2

    def halo(i, side):
        src, dst = fields[i]
        src_lo, dst_lo = ((0, HF + W), (W - HF, 0))[side]
        n, skip = (HF, 0) if i == 0 else (PART, core * PART)
        return pltpu.make_async_remote_copy(
            src_ref=src.at[pl.ds(src_lo + skip, n)], dst_ref=dst.at[pl.ds(dst_lo + skip, n)],
            send_sem=h_send.at[i, side], recv_sem=h_recv.at[i, side],
            device_id=(t, beside(2 * side - 1)), device_id_type=MESH)

    def share(i, side, which):
        dst = fields[i][1]
        part = dst.at[pl.ds((HF + W, 0)[side] + which * PART, PART)]
        return pltpu.make_async_remote_copy(
            src_ref=part, dst_ref=part, send_sem=m_send.at[i, side], recv_sem=m_recv.at[i, side],
            device_id=(mate, s), device_id_type=MESH)

    def halo2(side):
        src_lo, dst_lo = ((HF, HF + W), (W, 0))[side]
        return pltpu.make_async_remote_copy(
            src_ref=lv.at[4, pl.ds(src_lo, HF)], dst_ref=lv.at[4, pl.ds(dst_lo, HF)],
            send_sem=h2_send.at[side], recv_sem=h2_recv.at[side],
            device_id=(t, beside(2 * side - 1)), device_id_type=MESH)

    has_target = (s > 0, s < S - 1)
    far_first = sorted(range(S), key=lambda z: -min(z, S - z))
    order = (1, 2, 3, 4, 5, 0)
    for i in order:
        for side in (0, 1):
            pl.when(has_target[side])(lambda i=i, side=side: halo(i, side).start())

    for has, lo in ((s > 0, 0), (s < S - 1, HF + W)):
        @pl.when(jnp.logical_not(has))
        def _(lo=lo):
            edge = slice(lo, lo + HF)
            blank = jnp.zeros((HF, Z, Y), F32)
            for i in range(3):
                st[i, edge] = blank
            for i in range(2):
                ints[i, edge] = jnp.zeros((HF, Z, Y), jnp.int32)
            lv[0, edge] = blank
            lv[4, edge] = blank

    @pl.when(chain)
    def _():
        for n in range(GROUP):
            @pl.when(member(n) & (first + n != t))
            def _(n=n):
                pl.semaphore_signal(go, inc=1, device_id=(first + n, s), device_id_type=MESH)
        for has, lo in ((s > 1, 0), (s > 0, CW), (s < S - 1, 3 * CW), (s < S - 2, 4 * CW)):
            @pl.when(jnp.logical_not(has))
            def _(lo=lo):
                blank = jnp.zeros((CW, CZ, CY), F32)
                for i in range(5):
                    cs_win[i, lo : lo + CW] = blank

                for n in range(GROUP):
                    r_win[n, lo : lo + CW] = blank
                e_win[lo : lo + CW] = blank

    @pl.when(chain & short)
    def _():
        for lo in (0, WIN - CW // 2):
            for i in range(5):
                cs_win[i, lo : lo + CW // 2] = jnp.zeros((CW // 2, CZ, CY), F32)

    @pl.when(main)
    def _():
        margin = jnp.zeros((1, CZ, CY), F32)
        for lo in (0, S * CW + 1):
            for i in range(5):
                cs_full[i, lo : lo + 1] = margin
            for i in range(3):
                cur[i, lo : lo + 1] = margin
        for i in range(S):
            cur[0, 1 + i * CW : 1 + (i + 1) * CW] = jnp.zeros((CW, CZ, CY), F32)

    for copy in local:
        copy.wait()

    def widen(lo, n):
        own = slice(lo, lo + n)
        cls = ints[0, own]
        kappa = jnp.zeros(cls.shape, F32)
        for i in range(8):
            kappa = jnp.where(cls == i, kd[i], kappa)
        st[3, own] = kappa
        st[4, own] = ints[1, own].astype(F32)

    def sum_pairs(src, lo):
        for i in range(CW):
            pairs[i] = src[lo + 2 * i] + src[lo + 2 * i + 1]

    sum_pairs(lv.at[0], HF)
    s_own[...] = restrict(pairs[...])
    start_copy = pltpu.make_async_remote_copy(
        src_ref=s_own, dst_ref=s_next, send_sem=s_sem.at[0], recv_sem=s_sem.at[1],
        device_id=(lax.rem(t + T - 1, T), s), device_id_type=MESH)
    pl.when(t > 0)(lambda: start_copy.start())

    stat = [st.at[i] for i in range(5)]
    for lo, n in chunks(HF, HF + W, 2):
        widen(lo, n)

    def to_slab(src, dst_of, send, recv, step):
        return pltpu.make_async_remote_copy(
            src_ref=src, dst_ref=dst_of((2 - step) * CW), send_sem=send, recv_sem=recv,
            device_id=(t, beside(step)), device_id_type=MESH)

    steps = (-2, 2, -1, 1)

    def there(step):
        return (s + step >= 0) & (s + step < S)

    def cs_copy(j):
        return to_slab(cs_own, lambda lo: cs_win.at[:, pl.ds(lo, CW)],
                       c_send.at[j], c_recv.at[j], steps[j])

    def cs_half(j):
        lo = CW // 2 if steps[j] > 0 else 0
        return to_slab(cs_own.at[:, pl.ds(lo, CW // 2)],
                       lambda base: cs_win.at[:, pl.ds(base + lo, CW // 2)],
                       c_send.at[j], c_recv.at[j], steps[j])

    def cs_each(sending, act):
        for j in range(4):
            way = there(steps[j] if sending else -steps[j])
            if j < 2:
                pl.when(way & short)(lambda j=j: act(cs_half(j)))
                way = way & jnp.logical_not(short)
            pl.when(way)(lambda j=j: act(cs_copy(j)))

    @pl.when(chain | main | helper)
    def _():
        for i in range(5):
            sum_pairs(st.at[i], HF)
            cs_own[i] = restrict(pairs[...])

    @pl.when(chain)
    def _():
        for i in range(5):
            cs_win[i, 2 * CW : 3 * CW] = cs_own[i]
        cs_each(True, lambda copy: copy.start())

    for lo, n in chunks(HF + 1, HF + W - 1, 2):
        make_coefs(stat, coef, lo, n, 1.0)

    def f_copy(z):
        return pltpu.make_async_remote_copy(
            src_ref=cs_own, dst_ref=cs_full.at[:, pl.ds(1 + s * CW, CW)],
            send_sem=f_send.at[z], recv_sem=f_recv.at[s],
            device_id=(MAIN, z), device_id_type=MESH)

    def f_arrival(z):
        return pltpu.make_async_remote_copy(
            src_ref=cs_own, dst_ref=cs_full.at[:, pl.ds(1 + z * CW, CW)],
            send_sem=f_send.at[z], recv_sem=f_recv.at[z],
            device_id=(MAIN, z), device_id_type=MESH)

    def f_each(who, act):
        for z in range(S):
            gap = lax.rem(z - s + S, S)
            near = (gap <= 2) | (gap >= S - 2)
            wanted = jnp.logical_not(near) if who is helper else near & (gap != 0)
            pl.when(who & wanted)(lambda z=z: act(z))

    f_each(helper, lambda z: f_copy(z).start())

    @pl.when(main)
    def _():
        cs_full[:, pl.ds(1 + s * CW, CW)] = cs_own[...]

    def fine(src, dst, shift, lo, hi):
        for i, n in chunks(lo, hi, 2):
            dst[i - shift : i - shift + n] = stencil(coef, src, i, n)

    def inner(base):
        for j in range(1, HF + 1):
            last = base + j == 2 * HF
            dst, shift = (ends, HF) if last else (lv.at[base + j], 0)
            fine(lv.at[base + j - 1], dst, shift, HF + j, HF + W - j)

    def outer(base):
        for j in range(1, HF + 1):
            last = base + j == 2 * HF
            dst, shift = (ends, HF) if last else (lv.at[base + j], 0)
            fine(lv.at[base + j - 1], dst, shift, j, HF + j)
            fine(lv.at[base + j - 1], dst, shift, HF + W - j, E - j)

    inner(0)
    for i in order:
        for side in (0, 1):
            @pl.when(has_target[1 - side])
            def _(i=i, side=side):
                halo(i, side).wait_recv()
                if i > 0:
                    share(i, side, core).start()
    for i in order[:-1]:
        for side in (0, 1):
            pl.when(has_target[1 - side])(
                lambda i=i, side=side: share(i, side, 1 - core).wait_recv())
    for lo in (0, HF + W):
        for i, n in chunks(lo, lo + HF, 2):
            widen(i, n)
    for lo in (1, HF + W - 1):
        for i, n in chunks(lo, lo + HF, 2):
            make_coefs(stat, coef, i, n, 1.0)
    outer(0)
    for side in (0, 1):
        pl.when(has_target[side])(lambda side=side: halo2(side).start())

    f_each(main, lambda z: f_copy(z).start())
    inner(HF)

    @pl.when(chain)
    def _():
        cs_each(False, lambda copy: copy.wait_recv())
        cstat = [cs_win.at[i] for i in range(5)]
        for lo, n in chunks(1, WIN - 1, 4):
            make_coefs(cstat, ccoef, lo, n, 0.5)

    for side in (0, 1):
        pl.when(has_target[1 - side])(lambda side=side: halo2(side).wait_recv())
    outer(HF)

    pltpu.make_async_copy(ends, ends_out, loc_sem.at[0]).start()
    sum_pairs(ends, 0)
    pl.when(t < T - 1)(lambda: start_copy.wait_recv())
    pl.when(t != home)(lambda: pl.semaphore_wait(go, 1))

    def r_copy(n, kind, j):
        step = (0,) + steps
        step = step[j]
        size = CW if step == 0 or (abs(step) == 1 and kind < 2) else CW // 2
        lo = CW - size if step > 0 else 0
        return pltpu.make_async_remote_copy(
            src_ref=r_own.at[pl.ds(lo, size)],
            dst_ref=r_win.at[n, pl.ds((2 - step) * CW + lo, size)],
            send_sem=r_send.at[j], recv_sem=r_recv.at[n, j],
            device_id=(home, beside(step)), device_id_type=MESH)

    pieces = ((1, 2, 3, 4, 0), (3, 4, 0), (3, 4, 0), (0,))

    def r_each(act):
        for kind in range(TURNS):
            @pl.when(lax.rem(slot, TURNS) == kind)
            def _(kind=kind):
                r_pieces(slot, kind, act, False)

    def r_pieces(n, kind, act, wait):
        for j in pieces[kind]:
            step = ((0,) + steps)[j]
            other = (first + n != t) if wait else (home != t)
            condition = other if step == 0 else there(-step if wait else step)
            pl.when(condition)(lambda j=j: act(r_copy(n, kind, j)))

    @pl.when(t < T - 1)
    def _():
        r_own[...] = restrict(pairs[...]) - s_next[...]

        @pl.when(t == home)
        def _():
            r_win[slot, 2 * CW : 3 * CW] = r_own[...]
        r_each(lambda copy: copy.start())

    def d_copy(n):
        return pltpu.make_async_remote_copy(
            src_ref=d_out.at[n], dst_ref=d_in, send_sem=d_send.at[n], recv_sem=d_recv,
            device_id=(first + n, s), device_id_type=MESH)

    def e_copy(j):
        return to_slab(e_win.at[pl.ds(2 * CW, CW)], lambda lo: e_win.at[pl.ds(lo, CW)],
                       e_send.at[j], e_recv.at[j], steps[j])

    def p_copy(z):
        return pltpu.make_async_remote_copy(
            src_ref=p_own, dst_ref=p_full.at[served, pl.ds(s * CW, CW)],
            send_sem=p_send.at[z], recv_sem=p_recv.at[served, s],
            device_id=(MAIN, z), device_id_type=MESH)

    def p_arrival(x, z):
        return pltpu.make_async_remote_copy(
            src_ref=p_own, dst_ref=p_full.at[x, pl.ds(z * CW, CW)],
            send_sem=p_send.at[z], recv_sem=p_recv.at[x, z],
            device_id=(MAIN, z), device_id_type=MESH)

    def turn(n, src, dst):
        kind = n % TURNS
        lo, hi = 4 * kind, WIN - 4 * kind
        for j in range(1, 4):
            for i, m in chunks(lo + j, hi - j, CW):
                wb[1 - j % 2, i : i + m] = stencil(ccoef, src, i, m)
            src = wb.at[1 - j % 2]
        own_lo, own_hi = 2 * CW, 3 * CW
        d_out[n] = stencil(ccoef, src, own_lo, CW)
        pl.when(first + n != t)(lambda: d_copy(n).start())

        @pl.when(first + n == t)
        def _():
            d_in[...] = d_out[n]

        def arrivals():
            r_pieces(n, kind, lambda copy: copy.wait_recv(), True)

        if n == GROUP - 1:
            @pl.when(jnp.logical_not(final))
            def _():
                arrivals()
                p_own[...] = d_out[n] + r_win[n, own_lo:own_hi]
                for z in far_first:
                    p_copy(lax.rem(s + z, S)).start()
            return
        into = slice(own_lo, own_hi)
        arrivals()
        dst[into] = d_out[n] + r_win[n, into]
        for i, m in chunks(lo + 4, own_lo, CW) + chunks(own_hi, hi - 4, CW):
            dst[i : i + m] = stencil(ccoef, src, i, m) + r_win[n, i : i + m]

    @pl.when(chain)
    def _():
        @pl.when(jnp.logical_not(short))
        def _():
            r_pieces(0, 0, lambda copy: copy.wait_recv(), True)
            src = r_win.at[0]
            for n in range(1, HALF):
                turn(n, src, wb.at[1] if n < HALF - 1 else e_win)
                src = wb.at[1]
            for j in range(4):
                pl.when(there(steps[j]))(lambda j=j: e_copy(j).start())
            for j in range(4):
                pl.when(there(-steps[j]))(lambda j=j: e_copy(j).wait_recv())
            turn(HALF, e_win, wb.at[1])

        @pl.when(short)
        def _():
            r_pieces(HALF, 0, lambda copy: copy.wait_recv(), True)
            for i, m in chunks(4, WIN - 4, CW):
                wb[1, i : i + m] = r_win[HALF, i : i + m]

        for n in range(HALF + 1, GROUP):
            turn(n, wb.at[1], wb.at[1])

    def g_copy(m):
        return pltpu.make_async_remote_copy(
            src_ref=g_out.at[m], dst_ref=g_in, send_sem=g_send.at[m], recv_sem=g_recv,
            device_id=(m + HALF, s), device_id_type=MESH)

    @pl.when(main)
    def _():
        for z in range(S):
            pl.when(s != z)(lambda z=z: f_arrival(z).wait_recv())
        fstat = [cs_full.at[i] for i in range(5)]
        for lo, n in chunks(1, S * CW + 1, 4):
            make_coefs(fstat, fcoef, lo, n, 0.5)

        def big_turn(m, carry):
            @pl.when((m == 0) | (lax.rem(m, GROUP) == HALF))
            def _():
                x = (m + HALF) // GROUP
                for z in range(S):
                    p_arrival(x, z).wait_recv()
                for i, n in chunks(0, S * CW, CW):
                    cur[0, i + 1 : i + 1 + n] = cur[0, i + 1 : i + 1 + n] + p_full[x, i : i + n]

            for a, b in ((0, 1), (1, 2), (2, 1), (1, 0)):
                for i, n in chunks(1, S * CW + 1, CW):
                    cur[b, i : i + n] = stencil(fcoef, cur.at[a], i, n)
            g_out[m] = cur[0, pl.ds(1 + s * CW, CW)]
            pl.when(m + HALF != MAIN)(lambda: g_copy(m).start())
            return carry
        lax.fori_loop(0, T - HALF, big_turn, 0)

    start = (t == 0) | (t == HALF) | (slot == 0)
    pl.when(jnp.logical_not(start) & (t != home))(lambda: d_copy(slot).wait_recv())
    pl.when((t >= HALF) & (t != MAIN))(lambda: g_copy(t - HALF).wait_recv())

    @pl.when(main)
    def _():
        g_in[...] = g_out[MAIN - HALF]

    @pl.when(start)
    def _():
        d_in[...] = jnp.zeros((CW, CZ, CY), F32)

    @pl.when(t >= HALF)
    def _():
        d_in[...] = d_in[...] + g_in[...]

    delta_out[...] = d_in[...]
    pltpu.make_async_copy(ends, ends_out, loc_sem.at[0]).wait()

    for side in (0, 1):
        for i in order:
            pl.when(has_target[side])(lambda i=i, side=side: halo(i, side).wait_send())
            if i > 0:
                pl.when(has_target[1 - side])(
                    lambda i=i, side=side: share(i, side, core).wait_send())
        pl.when(has_target[side])(lambda side=side: halo2(side).wait_send())
    pl.when(t > 0)(lambda: start_copy.wait_send())
    pl.when(t < T - 1)(lambda: r_each(lambda copy: copy.wait_send()))

    @pl.when(chain)
    def _():
        for j in range(4):

            pl.when(there(steps[j]) & jnp.logical_not(short))(
                lambda j=j: e_copy(j).wait_send())
        cs_each(True, lambda copy: copy.wait_send())
        for n in range(1, GROUP):
            begun = jnp.logical_not(short) if n <= HALF else chain
            pl.when(begun & (first + n != t))(lambda n=n: d_copy(n).wait_send())

        @pl.when(t != LAST)
        def _():
            for z in range(S):
                p_copy(z).wait_send()

    f_each(helper, lambda z: f_copy(z).wait_send())
    f_each(main, lambda z: f_copy(z).wait_send())

    @pl.when(main)
    def _():
        def drain(m, carry):
            pl.when(m + HALF != MAIN)(lambda: g_copy(m).wait_send())
            return carry
        lax.fori_loop(0, T - HALF, drain, 0)


def correct(ends, delta, out):
    fine_delta = prolong(delta[...])
    for i in range(CW):
        out[2 * i] = ends[2 * i] + fine_delta[i]
        out[2 * i + 1] = ends[2 * i + 1] + fine_delta[i]


def shards(starts, u, w, v, cls, msk, kd):
    T, S = lax.axis_size("tm"), lax.axis_size("space")
    groups = T // GROUP + 1
    dma = pltpu.SemaphoreType.DMA
    anywhere = pl.BlockSpec(memory_space=pl.ANY)
    slab = (CW, CZ, CY)
    ends, delta = pl.pallas_call(
        functools.partial(kernel, T, S),
        out_shape=(jax.ShapeDtypeStruct((W, Z, Y), F32), jax.ShapeDtypeStruct(slab, F32)),
        in_specs=[anywhere] * 6 + [pl.BlockSpec(memory_space=pltpu.SMEM)],
        out_specs=(anywhere, pl.BlockSpec(memory_space=pltpu.VMEM)),
        scratch_shapes=[
            pltpu.VMEM((5, E, Z, Y), F32),
            pltpu.VMEM((2, E, Z, Y), jnp.int32),
            pltpu.VMEM((8, E, Z, Y), F32),
            pltpu.VMEM((7, E, Z, Y), F32),
            pltpu.VMEM((W, Z, Y), F32),
            pltpu.VMEM((CW, Z, Y), F32),
            pltpu.VMEM(slab, F32),
            pltpu.VMEM(slab, F32),
            pltpu.VMEM(slab, F32),
            pltpu.VMEM((5,) + slab, F32),
            pltpu.VMEM((5, WIN, CZ, CY), F32),
            pltpu.VMEM((7, WIN, CZ, CY), F32),
            pltpu.VMEM((GROUP, WIN, CZ, CY), F32),
            pltpu.VMEM((WIN, CZ, CY), F32),
            pltpu.VMEM((2, WIN, CZ, CY), F32),
            pltpu.VMEM((GROUP,) + slab, F32),
            pltpu.VMEM(slab, F32),
            pltpu.VMEM((5, S * CW + 2, CZ, CY), F32),
            pltpu.VMEM((7, S * CW + 2, CZ, CY), F32),
            pltpu.VMEM(slab, F32),
            pltpu.VMEM((groups - 1, S * CW, CZ, CY), F32),
            pltpu.VMEM((3, S * CW + 2, CZ, CY), F32),
            pltpu.VMEM((T - HALF,) + slab, F32),
            pltpu.VMEM(slab, F32),
            dma((6,)),
            dma((6, 2)), dma((6, 2)),
            dma((6, 2)), dma((6, 2)),
            dma((2,)), dma((2,)),
            dma((2,)),
            dma((5,)), dma((GROUP, 5)),
            dma((4,)), dma((4,)),
            dma((4,)), dma((4,)),
            dma((GROUP,)), dma(()),
            dma((S,)), dma((S,)),
            dma((S,)), dma((groups - 1, S)),
            dma((T - HALF,)), dma(()),
            pltpu.SemaphoreType.REGULAR,
        ],
        compiler_params=pltpu.CompilerParams(
            collective_id=0, has_side_effects=True, vmem_limit_bytes=56 * 1024 * 1024),
    )(starts[0], u, w, v, cls, msk, kd)
    vmem = pl.BlockSpec(memory_space=pltpu.VMEM)
    result = pl.pallas_call(
        correct, out_shape=jax.ShapeDtypeStruct((W, Z, Y), F32),
        in_specs=[vmem, vmem], out_specs=vmem)(ends, delta)
    return result[None]


def solution(mesh):
    slabs = P("space", None, None)
    return jax.shard_map(
        shards, mesh=mesh,
        in_specs=(P("tm", "space", None, None),) + (slabs,) * 5 + (P(),),
        out_specs=P("tm", "space", None, None), check_vma=False)
```
